128 devices in a mesh: pts: 8 (over x, core), shk: 16 (over z, y).
Axes of the slice: x: 4, y: 4, z: 4, core: 2. Of those that a mesh axis runs over, the one named last changes fastest.
Arguments:
- savings: float32 [16, 59, 1024], P('shk', None, 'pts'), may hold values from 0.05 to 0.95
- wealth: float32 [16, 59, 1024], P('shk', None, 'pts'), may hold values from 0.5 to 2
- surplus: bfloat16 [16, 118, 2048], P('shk', None, 'pts'), may hold values from -0.12 to 0.12
- point_dims: int32 [16, 3, 2048], P('shk', None, 'pts'), may hold values from 0 to 58
- point_levels: int32 [16, 3, 2048], P('shk', None, 'pts'), may hold values from 0 to 3
- point_index: int32 [16, 3, 2048], P('shk', None, 'pts'), may hold values from 1 to 7, as said below
- live_count: int32 [16, 8], P('shk', 'pts'), may hold values from 64 to 256
- trans_counts: int32 [16, 16], replicated, may hold values from 1 to 99
Outputs:
- savings_out: float32 [16, 59, 1024], P('shk', None, 'pts')
- consumption: float32 [16, 59, 1024], P('shk', None, 'pts')
The draws below stay inside these ranges and needn't reach their ends.
Inputs may be any that keep to these rules, and one draw needn't show every extreme that they name: `point_index`: odd, below 2 ** level where the level is positive, 1 where it is 0. Points at positions from live_count on in a shard are padding.
All inputs are finite; a program needn't handle non-finite values.
Results may differ from the reference program's by a relative error of at most 0.0011.
Values may be sent and summed in bfloat16 or wider, within the bound.
No kernel may reach another device: no remote copies, remote signals or barrier semaphores. Data moves between devices by JAX's collectives and lax.ppermute only.
A program may use at most 192 MiB of HBM per device.

```python
import jax
import jax.numpy as jnp
from jax import lax

DIM = 59
POL = 118
STATES = 16
ACTIVE = 3
LEVELS = 4
ITERS = 2
P_DEV = 256
POINTS = 2048
QUERIES = 1024
N_PTS = 8


def grid_pairs(key):
    inner = jax.random.fold_in(key, 7)
    first, second = jax.random.split(inner)
    shape = (STATES, ACTIVE, POINTS)
    levels = jax.random.randint(first, shape, 0, LEVELS)
    spans = jnp.left_shift(jnp.ones(shape, jnp.int32), jnp.maximum(levels - 1, 0))
    chosen = jax.random.randint(second, shape, 0, spans)
    return (levels.astype(jnp.int32), (2 * chosen + 1).astype(jnp.int32))


def draw_point_levels(key, part):
    return grid_pairs(key)[0]


def draw_point_index(key, part):
    return grid_pairs(key)[1]


def draw_surplus(key, part):
    inner = jax.random.fold_in(key, 11)
    first = jax.random.fold_in(inner, 0)
    shape = (STATES, POL, POINTS)
    values = 0.02 * jax.random.normal(first, shape, jnp.float32)
    return jnp.clip(values, -0.12, 0.12).astype(jnp.bfloat16)


def set_ends(entries, key, low, high):
    shape = entries.shape
    place = [jax.random.randint(jax.random.fold_in(key, axis), (), 0, shape[axis]) for axis in range(len(shape))]
    entries = entries.at[tuple(place)].set(low)
    longest = shape.index(max(shape))
    place[longest] = (place[longest] + 1) % shape[longest]
    return entries.at[tuple(place)].set(high)


def steps_of(stream_key, shape, cuts, least, top_value):
    def one(dim, blocks):
        draws = jax.random.uniform(jax.random.fold_in(jax.random.fold_in(stream_key, 6), dim), (blocks,), jnp.float32, least / len(cuts), top_value / len(cuts))
        return jnp.repeat(jnp.exp(draws), shape[dim] // blocks).reshape((-1,) + (1,) * (len(shape) - dim - 1))

    factor_of = one(*cuts[0])
    for cut in cuts[1:]:
        factor_of = factor_of * one(*cut)
    return factor_of


def setup_inputs(seed: int = 0) -> dict:
    splits = jax.random.split(jax.random.key(seed), 9)
    return {
        "savings": jnp.clip(0.05 + 0.9 * jax.random.uniform(splits[0], (STATES, DIM, QUERIES), jnp.float32) ** steps_of(splits[0], (STATES, DIM, QUERIES), ((0, 16), (2, 8)), -0.2, 0.2), 0.05, 0.95),
        "wealth": jnp.clip(0.5 + 1.5 * jax.random.uniform(splits[1], (STATES, DIM, QUERIES), jnp.float32) ** steps_of(splits[1], (STATES, DIM, QUERIES), ((0, 16), (2, 8)), -0.2, 0.2), 0.5, 2.0),
        "surplus": draw_surplus(jax.random.fold_in(splits[8], 71), 0),
        "point_dims": set_ends(jax.random.randint(splits[3], (STATES, ACTIVE, POINTS), 0, DIM), jax.random.fold_in(splits[3], 1), 0, DIM - 1).astype(jnp.int32),
        "point_levels": draw_point_levels(jax.random.fold_in(splits[8], 71), 0),
        "point_index": draw_point_index(jax.random.fold_in(splits[8], 71), 0),
        "live_count": set_ends(jax.random.randint(splits[6], (STATES, N_PTS), P_DEV // 4, P_DEV + 1), jax.random.fold_in(splits[6], 1), P_DEV // 4, P_DEV).astype(jnp.int32),
        "trans_counts": set_ends(jax.random.randint(splits[7], (STATES, STATES), 1, 100), jax.random.fold_in(splits[7], 1), 1, 99).astype(jnp.int32),
    }


GAMMA = 2.0
BETA = 0.96
damping = 0.5


def hat_tables(levels, indices):
    scaled = jnp.exp2(levels.astype(jnp.float32))
    inverse = jnp.where(levels > 0, scaled, jnp.zeros_like(scaled))
    centre = indices.astype(jnp.float32) / scaled
    return centre, inverse


def basis_block(coords, dims, centre, inverse):
    chosen = jnp.take(coords, dims, axis=0)
    factor = jnp.maximum(0.0, 1.0 - jnp.abs(chosen - centre[:, :, None]) * inverse[:, :, None])
    product = factor[0]
    for slot in range(1, factor.shape[0]):
        product = product * factor[slot]
    return product.astype(jnp.bfloat16)


def reference(savings, wealth, surplus, point_dims, point_levels, point_index, live_count, trans_counts):
    counts = trans_counts.astype(jnp.float32)
    prob = counts / jnp.sum(counts, axis=1, keepdims=True)
    centre, inverse = hat_tables(point_levels, point_index)
    position = jnp.arange(POINTS, dtype=jnp.int32)
    shard = (position // P_DEV).astype(jnp.int32)
    limit = jnp.take(live_count, shard, axis=1)
    within = (position % P_DEV).astype(jnp.int32)
    live_surplus = jnp.where(within[None, None, :] < limit[:, None, :], surplus, jnp.zeros_like(surplus))
    current = savings
    consumption = savings
    for sweep in range(ITERS):
        rounded = lax.optimization_barrier(current.astype(jnp.bfloat16)).astype(jnp.float32)

        def one_state(tables):
            weights, dims, cen, inv = tables

            def one_block(coords):
                basis = basis_block(coords, dims, cen, inv)
                return jnp.dot(weights, basis, preferred_element_type=jnp.float32)

            return lax.map(one_block, rounded)

        interp = lax.map(one_state, (live_surplus, point_dims, centre, inverse))
        marginal = jnp.exp(-GAMMA * interp[:, :, :DIM] + interp[:, :, DIM:])
        expect = jnp.einsum("ab,badq->adq", prob, marginal, precision=lax.Precision.HIGHEST)
        consumption = (BETA * expect) ** (-1.0 / GAMMA)
        current = (1.0 - damping) * current + damping * jax.nn.sigmoid(wealth - consumption)
    return current, consumption
```

```python
import functools

import jax
import jax.numpy as jnp
from jax import lax
from jax.experimental import pallas as pl
from jax.experimental.pallas import tpu as pltpu
from jax.sharding import PartitionSpec as P

ITERS = 2
GAMMA = 2.0
BETA = 0.96
damping = 0.5
DIM = 59
HALF = 64
RING = 4
BF = jnp.bfloat16
F32 = jnp.float32


def pack(surplus, dims, levels, index, live):
    npoints = surplus.shape[1]
    position = lax.iota(jnp.int32, npoints)
    kept = jnp.where(position[None, :] < live, surplus, jnp.zeros_like(surplus))
    refined = levels > 0
    scale = jnp.where(refined, jnp.exp2(levels.astype(F32)), 0.0).astype(BF)
    bias = jnp.where(refined, 1 - index, 1).astype(BF)
    which = dims.astype(BF)
    return jnp.concatenate(
        [kept[:DIM], which, scale[:2], kept[DIM:], scale[2:], bias, jnp.zeros((1, npoints), BF)], axis=0
    )


def kernel(where_ref, counts_ref, tab_ref, q0, q1, q2, q3, o0, o1, o2, o3, qt_ref, acc_ref, sum_ref):
    z, y = where_ref[0], where_ref[1]
    for j, q in enumerate((q0, q1, q2, q3)):
        qt_ref[pl.ds(j * 128, 128), :] = q[...].astype(F32).T.astype(BF)
    row = lax.broadcasted_iota(jnp.int32, (HALF, 256), 0)
    for yy in range(RING):
        acc_ref[...] = jnp.zeros_like(acc_ref)

        @pl.loop(0, 8)
        def _(p):
            blk = tab_ref[p * RING + yy]
            par = jnp.concatenate([blk[56:64], blk[120:128]], axis=0).astype(F32)
            basis = None
            for k in range(3):
                dim = par[3 + k : 4 + k].astype(jnp.int32)
                scale = par[6 + k : 7 + k] if k < 2 else par[11:12]
                bias = par[12 + k : 13 + k]
                table = jnp.where(row == dim, scale, jnp.where(row == DIM, bias, 0.0)).astype(BF)
                left = jnp.dot(qt_ref[...], table, preferred_element_type=F32)
                factor = jnp.maximum(jnp.minimum(left, 2.0 - left), 0.0)
                basis = factor if basis is None else basis * factor
            acc_ref[...] += lax.dot_general(
                basis.astype(BF), blk, (((1,), (1,)), ((), ())), preferred_element_type=F32
            )

        value = acc_ref[...]
        marginal = jnp.exp(-GAMMA * value[:, :HALF] + value[:, HALF:])
        for j in range(RING):
            s = lax.rem(z + j, RING) * RING + y
            count = counts_ref[s, z * RING + yy].astype(F32)
            term = count * marginal[j * 128 : (j + 1) * 128]
            if yy == 0:
                sum_ref[j] = term
            else:
                sum_ref[j] += term
    for j, o in enumerate((o0, o1, o2, o3)):
        o[...] = sum_ref[j].T


def partial_sums(where, counts, tables, queries):
    vm = pl.BlockSpec(memory_space=pltpu.VMEM)
    sm = pl.BlockSpec(memory_space=pltpu.SMEM)
    return pl.pallas_call(
        kernel,
        out_shape=[jax.ShapeDtypeStruct((HALF, 128), F32)] * RING,
        in_specs=[sm, sm, vm, vm, vm, vm, vm],
        out_specs=[vm] * RING,
        scratch_shapes=[
            pltpu.VMEM((512, HALF), BF),
            pltpu.VMEM((512, 128), F32),
            pltpu.VMEM((RING, 128, HALF), F32),
        ],
        compiler_params=pltpu.CompilerParams(vmem_limit_bytes=40 << 20),
        name="euler_basis",
    )(where, counts, tables, *queries)


def shift(dz):
    return [(z * RING + y, (z + dz) % RING * RING + y) for z in range(RING) for y in range(RING)]


def per_device(savings, wealth, surplus, point_dims, point_levels, point_index, live_count, trans_counts):
    block = pack(surplus[0], point_dims[0], point_levels[0], point_index[0], live_count[0, 0])
    groups = [
        [p * 16 + z * RING + y for p in range(8) for y in range(RING)] for z in range(RING)
    ]
    tables = lax.all_to_all(
        jnp.broadcast_to(block[None], (32,) + block.shape), ("pts", "shk"), 0, 0, tiled=True, axis_index_groups=groups
    )
    shock = lax.axis_index("shk")
    where = jnp.stack([shock // RING, shock % RING]).astype(jnp.int32)
    rowsum = jnp.sum(lax.dynamic_index_in_dim(trans_counts, shock, 0, keepdims=False).astype(F32))
    current = savings[0]
    income = wealth[0]
    nq = current.shape[1]
    consumption = current
    for sweep in range(ITERS):
        own = jnp.concatenate(
            [current.astype(BF), jnp.ones((1, nq), BF), jnp.zeros((HALF - DIM - 1, nq), BF)], axis=0
        )
        queries = [own] + [lax.ppermute(own, "shk", shift(-j)) for j in range(1, RING)]
        parts = partial_sums(where, trans_counts, tables, queries)
        got = [parts[0]] + [lax.ppermute(parts[j], "shk", shift(j)) for j in range(1, RING)]
        expect = ((got[0] + got[1]) + (got[2] + got[3]))[:DIM] / rowsum
        consumption = (BETA * expect) ** (-1.0 / GAMMA)
        current = (1.0 - damping) * current + damping * jax.nn.sigmoid(income - consumption)
    return (current[None], consumption[None])


def solution(mesh):
    return jax.shard_map(
        per_device,
        mesh=mesh,
        in_specs=(
            P("shk", None, "pts"),
            P("shk", None, "pts"),
            P("shk", None, "pts"),
            P("shk", None, "pts"),
            P("shk", None, "pts"),
            P("shk", None, "pts"),
            P("shk", "pts"),
            P(),
        ),
        out_specs=(P("shk", None, "pts"), P("shk", None, "pts")),
        check_vma=False,
    )
```

```python
import functools

import jax
import jax.numpy as jnp
from jax import lax
from jax.experimental import pallas as pl
from jax.experimental.pallas import tpu as pltpu
from jax.sharding import PartitionSpec as P

ITERS = 2
GAMMA = 2.0
BETA = 0.96
damping = 0.5
DIM = 59
HALF = 64
RING = 4
UNIT = 2
BF = jnp.bfloat16
F32 = jnp.float32


def pack(surplus, dims, levels, index, live):
    npoints = surplus.shape[1]
    position = lax.iota(jnp.int32, npoints)
    kept = jnp.where(position[None, :] < live, surplus, jnp.zeros_like(surplus))
    refined = levels > 0
    scale = jnp.where(refined, jnp.exp2(levels.astype(F32)), 0.0).astype(BF)
    bias = jnp.where(refined, 1 - index, 1).astype(BF)
    which = dims.astype(BF)
    return jnp.concatenate(
        [kept[:DIM], which, scale[:2], kept[DIM:], scale[2:], bias, jnp.zeros((1, npoints), BF)], axis=0
    )


def kernel(
    where_ref, counts_ref, tab_ref, q0, q1, q2, q3, o0, o1, o2, o3, qt_ref, sel_a, sel_b, basis_a, basis_b, acc_ref
):
    z, y = where_ref[0], where_ref[1]
    for j, q in enumerate((q0, q1, q2, q3)):
        qt_ref[pl.ds(j * 128, 128), :] = q[...].astype(F32).T.astype(BF)
    row = lax.broadcasted_iota(jnp.int32, (HALF, 256), 0)
    units = 8 * RING // UNIT

    def block(i):
        return tab_ref[(i % 8) * RING + i // 8]

    def select(u, sel_ref):
        for b in range(UNIT):
            blk = block(jnp.minimum(u, units - 1) * UNIT + b)
            par = jnp.concatenate([blk[56:64], blk[120:128]], axis=0).astype(F32)
            for k in range(3):
                dim = par[3 + k : 4 + k].astype(jnp.int32)
                scale = par[6 + k : 7 + k] if k < 2 else par[11:12]
                bias = par[12 + k : 13 + k]
                table = jnp.where(row == dim, scale, jnp.where(row == DIM, bias, 0.0))
                sel_ref[b, k] = table.astype(BF)

    def hats(sel_ref, basis_ref):
        for b in range(UNIT):
            basis = None
            for k in range(3):
                left = jnp.dot(qt_ref[...], sel_ref[b, k], preferred_element_type=F32)
                factor = jnp.maximum(jnp.minimum(left, 2.0 - left), 0.0)
                basis = factor if basis is None else basis * factor
            basis_ref[:, pl.ds(b * 256, 256)] = basis.astype(BF)

    def sums(u, basis_ref):
        weights = jnp.concatenate([block(u * UNIT + b) for b in range(UNIT)], axis=1)
        acc_ref[u * UNIT // 8] += lax.dot_general(
            basis_ref[...], weights, (((1,), (1,)), ((), ())), preferred_element_type=F32
        )

    acc_ref[...] = jnp.zeros_like(acc_ref)
    select(0, sel_a)
    select(1, sel_b)
    hats(sel_a, basis_a)
    select(2, sel_a)

    @pl.loop(0, units // 2 - 1)
    def _(it):
        u = 2 * it + 1
        hats(sel_b, basis_b)
        sums(u - 1, basis_a)
        select(u + 2, sel_b)
        hats(sel_a, basis_a)
        sums(u, basis_b)
        select(u + 3, sel_a)

    hats(sel_b, basis_b)
    sums(units - 2, basis_a)
    sums(units - 1, basis_b)

    for j, o in enumerate((o0, o1, o2, o3)):
        s = lax.rem(z + j, RING) * RING + y
        total = None
        for t in range(RING):
            value = acc_ref[t, pl.ds(j * 128, 128), :]
            count = counts_ref[s, z * RING + t].astype(F32)
            term = count * jnp.exp(-GAMMA * value[:, :HALF] + value[:, HALF:])
            total = term if total is None else total + term
        o[...] = total.T


def partial_sums(where, counts, tables, queries):
    vm = pl.BlockSpec(memory_space=pltpu.VMEM)
    sm = pl.BlockSpec(memory_space=pltpu.SMEM)
    return pl.pallas_call(
        kernel,
        out_shape=[jax.ShapeDtypeStruct((HALF, 128), F32)] * RING,
        in_specs=[sm, sm, vm, vm, vm, vm, vm],
        out_specs=[vm] * RING,
        scratch_shapes=[
            pltpu.VMEM((512, HALF), BF),
            pltpu.VMEM((UNIT, 3, HALF, 256), BF),
            pltpu.VMEM((UNIT, 3, HALF, 256), BF),
            pltpu.VMEM((512, UNIT * 256), BF),
            pltpu.VMEM((512, UNIT * 256), BF),
            pltpu.VMEM((RING, 512, 128), F32),
        ],
        compiler_params=pltpu.CompilerParams(vmem_limit_bytes=40 << 20),
        name="euler_basis",
    )(where, counts, tables, *queries)


def shift(dz):
    return [(z * RING + y, (z + dz) % RING * RING + y) for z in range(RING) for y in range(RING)]


def per_device(savings, wealth, surplus, point_dims, point_levels, point_index, live_count, trans_counts):
    block = pack(surplus[0], point_dims[0], point_levels[0], point_index[0], live_count[0, 0])
    groups = [
        [p * 16 + z * RING + y for p in range(8) for y in range(RING)] for z in range(RING)
    ]
    tables = lax.all_to_all(
        jnp.broadcast_to(block[None], (32,) + block.shape), ("pts", "shk"), 0, 0, tiled=True, axis_index_groups=groups
    )
    shock = lax.axis_index("shk")
    where = jnp.stack([shock // RING, shock % RING]).astype(jnp.int32)
    rowsum = jnp.sum(lax.dynamic_index_in_dim(trans_counts, shock, 0, keepdims=False).astype(F32))
    current = savings[0]
    income = wealth[0]
    nq = current.shape[1]
    consumption = current
    for sweep in range(ITERS):
        own = jnp.concatenate(
            [current.astype(BF), jnp.ones((1, nq), BF), jnp.zeros((HALF - DIM - 1, nq), BF)], axis=0
        )
        queries = [own] + [lax.ppermute(own, "shk", shift(-j)) for j in range(1, RING)]
        parts = partial_sums(where, trans_counts, tables, queries)
        got = [parts[0]] + [lax.ppermute(parts[j], "shk", shift(j)) for j in range(1, RING)]
        expect = ((got[0] + got[1]) + (got[2] + got[3]))[:DIM] / rowsum
        consumption = (BETA * expect) ** (-1.0 / GAMMA)
        current = (1.0 - damping) * current + damping * jax.nn.sigmoid(income - consumption)
    return (current[None], consumption[None])


def solution(mesh):
    return jax.shard_map(
        per_device,
        mesh=mesh,
        in_specs=(
            P("shk", None, "pts"),
            P("shk", None, "pts"),
            P("shk", None, "pts"),
            P("shk", None, "pts"),
            P("shk", None, "pts"),
            P("shk", None, "pts"),
            P("shk", "pts"),
            P(),
        ),
        out_specs=(P("shk", None, "pts"), P("shk", None, "pts")),
        check_vma=False,
    )
```

```python
import jax
import jax.numpy as jnp
from jax import lax
from jax.experimental import pallas as pl
from jax.experimental.pallas import tpu as pltpu
from jax.sharding import PartitionSpec as P

ITERS = 2
GAMMA = 2.0
BETA = 0.96
damping = 0.5
DIM = 59
HALF = 64
RING = 4
UNIT = 2
BF = jnp.bfloat16
F32 = jnp.float32


def pack_kernel(live_ref, surplus_ref, dims_ref, levels_ref, index_ref, o_ref):
    npoints = surplus_ref.shape[1]
    position = lax.broadcasted_iota(jnp.int32, (1, npoints), 1)
    kept = position < live_ref[0, 0]
    body = jnp.where(kept, surplus_ref[0:112, :].astype(F32), 0.0).astype(BF)
    row = lax.broadcasted_iota(jnp.int32, (16, npoints), 0)
    tail = jnp.where(kept, surplus_ref[112:118, :].astype(F32), 0.0)
    tail = jnp.concatenate([tail, jnp.zeros((10, npoints), F32)], axis=0)
    for k in range(3):
        level = levels_ref[k]
        refined = level > 0
        scale = jnp.where(refined, jnp.left_shift(jnp.ones_like(level), level), 0).astype(F32)
        bias = jnp.where(refined, 1 - index_ref[k], 1).astype(F32)
        for place, value in ((6 + k, dims_ref[k].astype(F32)), (9 + k, scale), (12 + k, bias)):
            tail = jnp.where(row == place, value, tail)
    tail = tail.astype(BF)
    for g in range(o_ref.shape[0]):
        o_ref[g, 0:112, :] = body
        o_ref[g, 112:128, :] = tail


def pack(surplus, dims, levels, index, live):
    vm = pl.BlockSpec(memory_space=pltpu.VMEM)
    sm = pl.BlockSpec(memory_space=pltpu.SMEM)
    return pl.pallas_call(
        pack_kernel,
        out_shape=jax.ShapeDtypeStruct((16, 128, surplus.shape[1]), BF),
        in_specs=[sm, vm, vm, vm, vm],
        out_specs=vm,
        compiler_params=pltpu.CompilerParams(vmem_limit_bytes=8 << 20),
        name="pack_tables",
    )(live, surplus, *(jnp.transpose(v, (1, 0, 2)) for v in (dims, levels, index)))


def finish_kernel(rowsum_ref, now_ref, income_ref, g0, g1, g2, g3, cur_ref, con_ref):
    total = ((g0[...] + g1[...]) + (g2[...] + g3[...]))[:DIM]
    expect = total / rowsum_ref[0].astype(F32)
    consumption = (BETA * expect) ** (-1.0 / GAMMA)
    value = income_ref[:, 0, :] - consumption
    share = 1.0 / (1.0 + jnp.exp(-value))
    con_ref[:, 0, :] = consumption
    cur_ref[:, 0, :] = (1.0 - damping) * now_ref[...] + damping * share


def finish(rowsum, current, income, got):
    vm = pl.BlockSpec(memory_space=pltpu.VMEM)
    sm = pl.BlockSpec(memory_space=pltpu.SMEM)
    flat = jax.ShapeDtypeStruct((DIM, 1, current.shape[1]), F32)
    new, consumption = pl.pallas_call(
        finish_kernel,
        out_shape=[flat, flat],
        in_specs=[sm, vm, vm, vm, vm, vm, vm],
        out_specs=[vm, vm],
        compiler_params=pltpu.CompilerParams(vmem_limit_bytes=4 << 20),
        name="finish",
    )(rowsum, current, income, *got)
    return jnp.transpose(new, (1, 0, 2)), jnp.transpose(consumption, (1, 0, 2))


def kernel(
    where_ref, counts_ref, tab_a, tab_b, q0, q1, q2, q3, o0, o1, o2, o3, qt_ref, sel_a, sel_b, basis_a, basis_b, acc_ref
):
    z, y = where_ref[0], where_ref[1]
    for j, q in enumerate((q0, q1, q2, q3)):
        qt_ref[pl.ds(j * 128, 128), :] = q[...].astype(F32).T.astype(BF)
    row = lax.broadcasted_iota(jnp.int32, (HALF, 256), 0)
    units = 8 * RING // UNIT

    def block(u, b):
        return (tab_a, tab_b)[b][(u % RING) * RING + u // RING]

    def select(u, sel_ref):
        for b in range(UNIT):
            par = block(jnp.minimum(u, units - 1), b)[112:128].astype(F32)
            for k in range(3):
                dim = par[6 + k : 7 + k].astype(jnp.int32)
                scale = par[9 + k : 10 + k]
                bias = par[12 + k : 13 + k]
                table = jnp.where(row == dim, scale, jnp.where(row == DIM, bias, 0.0))
                sel_ref[b, k] = table.astype(BF)

    def hats(sel_ref, basis_ref):
        for b in range(UNIT):
            basis = None
            for k in range(3):
                left = jnp.dot(qt_ref[...], sel_ref[b, k], preferred_element_type=F32)
                factor = jnp.maximum(jnp.minimum(left, 2.0 - left), 0.0)
                basis = factor if basis is None else basis * factor
            basis_ref[:, pl.ds(b * 256, 256)] = basis.astype(BF)

    def sums(u, basis_ref):
        weights = jnp.concatenate([block(u, b) for b in range(UNIT)], axis=1)
        acc_ref[u // RING] += lax.dot_general(
            basis_ref[...], weights, (((1,), (1,)), ((), ())), preferred_element_type=F32
        )

    acc_ref[...] = jnp.zeros_like(acc_ref)
    select(0, sel_a)
    select(1, sel_b)
    hats(sel_a, basis_a)
    select(2, sel_a)

    @pl.loop(0, units // 2 - 1)
    def _(it):
        u = 2 * it + 1
        hats(sel_b, basis_b)
        sums(u - 1, basis_a)
        select(u + 2, sel_b)
        hats(sel_a, basis_a)
        sums(u, basis_b)
        select(u + 3, sel_a)

    hats(sel_b, basis_b)
    sums(units - 2, basis_a)
    sums(units - 1, basis_b)

    for j, o in enumerate((o0, o1, o2, o3)):
        s = lax.rem(z + j, RING) * RING + y
        total = None
        for t in range(RING):
            value = acc_ref[t, pl.ds(j * 128, 128), :]
            count = counts_ref[s, z * RING + t].astype(F32)
            term = count * jnp.exp(-GAMMA * value + pltpu.roll(value, 128 - DIM, 1))
            total = term if total is None else total + term
        o[...] = total.T[:HALF]


def partial_sums(where, counts, tables, queries):
    vm = pl.BlockSpec(memory_space=pltpu.VMEM)
    sm = pl.BlockSpec(memory_space=pltpu.SMEM)
    return pl.pallas_call(
        kernel,
        out_shape=[jax.ShapeDtypeStruct((HALF, 128), F32)] * RING,
        in_specs=[sm, sm] + [vm] * 6,
        out_specs=[vm] * RING,
        scratch_shapes=[
            pltpu.VMEM((512, HALF), BF),
            pltpu.VMEM((UNIT, 3, HALF, 256), BF),
            pltpu.VMEM((UNIT, 3, HALF, 256), BF),
            pltpu.VMEM((512, UNIT * 256), BF),
            pltpu.VMEM((512, UNIT * 256), BF),
            pltpu.VMEM((RING, 512, 128), F32),
        ],
        compiler_params=pltpu.CompilerParams(vmem_limit_bytes=40 << 20),
        name="euler_basis",
    )(where, counts, *tables, *queries)


def shift(dz):
    return [(z * RING + y, (z + dz) % RING * RING + y) for z in range(RING) for y in range(RING)]


def spread(current):
    nq = current.shape[1]
    own = jnp.concatenate([current.astype(BF), jnp.ones((1, nq), BF), jnp.zeros((HALF - DIM - 1, nq), BF)], axis=0)
    return [own] + [lax.ppermute(own, "shk", shift(-j)) for j in range(1, RING)]


def per_device(savings, wealth, surplus, point_dims, point_levels, point_index, live_count, trans_counts):
    blocks = pack(surplus[0], point_dims, point_levels, point_index, live_count)
    groups = [
        [(2 * x + c) * 16 + z * RING + y for x in range(RING) for y in range(RING)] for c in range(2) for z in range(RING)
    ]
    mine = lax.all_to_all(blocks, ("pts", "shk"), 0, 0, tiled=True, axis_index_groups=groups)
    current = savings[0]
    income = wealth[0]
    queries = spread(current)
    mine, *queries = lax.optimization_barrier((mine, *queries))
    tables = (mine, lax.ppermute(mine, "pts", [(i, i ^ 1) for i in range(8)]))
    shock = lax.axis_index("shk")
    where = jnp.stack([shock // RING, shock % RING]).astype(jnp.int32)
    rowsum = jnp.sum(lax.dynamic_index_in_dim(trans_counts, shock, 0, keepdims=False))
    for sweep in range(ITERS):
        if sweep:
            queries = spread(current)
        parts = partial_sums(where, trans_counts, tables, queries)
        got = [parts[0]] + [lax.ppermute(parts[j], "shk", shift(j)) for j in range(1, RING)]
        if sweep == ITERS - 1:
            return finish(rowsum[None], current, jnp.transpose(wealth, (1, 0, 2)), got)
        expect = ((got[0] + got[1]) + (got[2] + got[3]))[:DIM] / rowsum.astype(F32)
        consumption = (BETA * expect) ** (-1.0 / GAMMA)
        current = (1.0 - damping) * current + damping * jax.nn.sigmoid(income - consumption)


def solution(mesh):
    return jax.shard_map(
        per_device,
        mesh=mesh,
        in_specs=(
            P("shk", None, "pts"),
            P("shk", None, "pts"),
            P("shk", None, "pts"),
            P("shk", None, "pts"),
            P("shk", None, "pts"),
            P("shk", None, "pts"),
            P("shk", "pts"),
            P(),
        ),
        out_specs=(P("shk", None, "pts"), P("shk", None, "pts")),
        check_vma=False,
    )
```

```python
import jax
import jax.numpy as jnp
from jax import lax
from jax.experimental import pallas as pl
from jax.experimental.pallas import tpu as pltpu
from jax.sharding import PartitionSpec as P

ITERS = 2
GAMMA = 2.0
BETA = 0.96
damping = 0.5
DIM = 59
HALF = 64
RING = 4
UNIT = 2
BF = jnp.bfloat16
F32 = jnp.float32
F8 = jnp.float8_e4m3fn
SPLIT = 32.0


def pack_kernel(live_ref, surplus_ref, dims_ref, levels_ref, index_ref, o_ref):
    npoints = surplus_ref.shape[1]
    position = lax.broadcasted_iota(jnp.int32, (1, npoints), 1)
    kept = position < live_ref[0, 0]
    body = jnp.where(kept, surplus_ref[0:112, :].astype(F32), 0.0).astype(BF)
    row = lax.broadcasted_iota(jnp.int32, (16, npoints), 0)
    tail = jnp.where(kept, surplus_ref[112:118, :].astype(F32), 0.0)
    tail = jnp.concatenate([tail, jnp.zeros((10, npoints), F32)], axis=0)
    for k in range(3):
        level = levels_ref[k]
        refined = level > 0
        scale = jnp.where(refined, jnp.left_shift(jnp.ones_like(level), level), 0).astype(F32)
        bias = jnp.where(refined, 1 - index_ref[k], 1).astype(F32)
        for place, value in ((6 + k, dims_ref[k].astype(F32)), (9 + k, scale), (12 + k, bias)):
            tail = jnp.where(row == place, value, tail)
    tail = tail.astype(BF)
    for g in range(o_ref.shape[0]):
        o_ref[g, 0:112, :] = body
        o_ref[g, 112:128, :] = tail


def pack(surplus, dims, levels, index, live):
    vm = pl.BlockSpec(memory_space=pltpu.VMEM)
    sm = pl.BlockSpec(memory_space=pltpu.SMEM)
    return pl.pallas_call(
        pack_kernel,
        out_shape=jax.ShapeDtypeStruct((16, 128, surplus.shape[1]), BF),
        in_specs=[sm, vm, vm, vm, vm],
        out_specs=vm,
        compiler_params=pltpu.CompilerParams(vmem_limit_bytes=8 << 20),
        name="pack_tables",
    )(live, surplus, *(jnp.transpose(v, (1, 0, 2)) for v in (dims, levels, index)))


def finish_kernel(rowsum_ref, now_ref, income_ref, g0, g1, g2, g3, cur_ref, con_ref):
    total = ((g0[...] + g1[...]) + (g2[...] + g3[...]))[:DIM]
    expect = total / rowsum_ref[0].astype(F32)
    consumption = (BETA * expect) ** (-1.0 / GAMMA)
    value = income_ref[:, 0, :] - consumption
    share = 1.0 / (1.0 + jnp.exp(-value))
    con_ref[:, 0, :] = consumption
    cur_ref[:, 0, :] = (1.0 - damping) * now_ref[...] + damping * share


def finish(rowsum, current, income, got):
    vm = pl.BlockSpec(memory_space=pltpu.VMEM)
    sm = pl.BlockSpec(memory_space=pltpu.SMEM)
    flat = jax.ShapeDtypeStruct((DIM, 1, current.shape[1]), F32)
    new, consumption = pl.pallas_call(
        finish_kernel,
        out_shape=[flat, flat],
        in_specs=[sm, vm, vm, vm, vm, vm, vm],
        out_specs=[vm, vm],
        compiler_params=pltpu.CompilerParams(vmem_limit_bytes=4 << 20),
        name="finish",
    )(rowsum, current, income, *got)
    return jnp.transpose(new, (1, 0, 2)), jnp.transpose(consumption, (1, 0, 2))


def kernel(
    where_ref, counts_ref, tab_a, tab_b, q0, q1, q2, q3, o0, o1, o2, o3, qt_ref, sel_a, sel_b, basis_a, basis_b, acc_ref
):
    z, y = where_ref[0], where_ref[1]
    for j, q in enumerate((q0, q1, q2, q3)):
        whole = q[...].astype(F32)
        whole = jnp.where(lax.broadcasted_iota(jnp.int32, whole.shape, 0) < DIM, whole * SPLIT, whole)
        high = whole.astype(F8).astype(F32)
        qt_ref[pl.ds(j * 128, 128), :] = jnp.concatenate([high, whole - high], axis=0).T.astype(F8)
    row = lax.broadcasted_iota(jnp.int32, (2 * HALF, 256), 0)
    coord = row % HALF
    units = 8 * RING // UNIT

    def block(u, b):
        return (tab_a, tab_b)[b][(u % RING) * RING + u // RING]

    def select(u, sel_ref):
        for b in range(UNIT):
            par = block(jnp.minimum(u, units - 1), b)[112:128].astype(F32)
            for k in range(3):
                dim = par[6 + k : 7 + k].astype(jnp.int32)
                scale = par[9 + k : 10 + k] * (1.0 / SPLIT)
                bias = par[12 + k : 13 + k]
                table = jnp.where(coord == dim, scale, jnp.where(row == DIM, bias, 0.0))
                sel_ref[b, k] = table.astype(F8)

    def hats(sel_ref, basis_ref):
        for b in range(UNIT):
            basis = None
            for k in range(3):
                left = jnp.dot(qt_ref[...], sel_ref[b, k], preferred_element_type=F32).astype(BF)
                factor = jnp.maximum(jnp.minimum(left, BF(2.0) - left), BF(0.0))
                basis = factor if basis is None else basis * factor
            basis_ref[:, pl.ds(b * 256, 256)] = basis

    def sums(u, basis_ref):
        weights = jnp.concatenate([block(u, b) for b in range(UNIT)], axis=1)
        acc_ref[u // RING] += lax.dot_general(
            basis_ref[...], weights, (((1,), (1,)), ((), ())), preferred_element_type=F32
        )

    acc_ref[...] = jnp.zeros_like(acc_ref)
    select(0, sel_a)
    select(1, sel_b)
    hats(sel_a, basis_a)
    select(2, sel_a)

    @pl.loop(0, units // 2 - 1)
    def _(it):
        u = 2 * it + 1
        hats(sel_b, basis_b)
        sums(u - 1, basis_a)
        select(u + 2, sel_b)
        hats(sel_a, basis_a)
        sums(u, basis_b)
        select(u + 3, sel_a)

    hats(sel_b, basis_b)
    sums(units - 2, basis_a)
    sums(units - 1, basis_b)

    for j, o in enumerate((o0, o1, o2, o3)):
        s = lax.rem(z + j, RING) * RING + y
        total = None
        for t in range(RING):
            value = acc_ref[t, pl.ds(j * 128, 128), :]
            count = counts_ref[s, z * RING + t].astype(F32)
            term = count * jnp.exp(-GAMMA * value + pltpu.roll(value, 128 - DIM, 1))
            total = term if total is None else total + term
        o[...] = total.T[:HALF]


def partial_sums(where, counts, tables, queries):
    vm = pl.BlockSpec(memory_space=pltpu.VMEM)
    sm = pl.BlockSpec(memory_space=pltpu.SMEM)
    return pl.pallas_call(
        kernel,
        out_shape=[jax.ShapeDtypeStruct((HALF, 128), F32)] * RING,
        in_specs=[sm, sm] + [vm] * 6,
        out_specs=[vm] * RING,
        scratch_shapes=[
            pltpu.VMEM((512, 2 * HALF), F8),
            pltpu.VMEM((UNIT, 3, 2 * HALF, 256), F8),
            pltpu.VMEM((UNIT, 3, 2 * HALF, 256), F8),
            pltpu.VMEM((512, UNIT * 256), BF),
            pltpu.VMEM((512, UNIT * 256), BF),
            pltpu.VMEM((RING, 512, 128), F32),
        ],
        compiler_params=pltpu.CompilerParams(vmem_limit_bytes=40 << 20),
        name="euler_basis",
    )(where, counts, *tables, *queries)


def shift(dz):
    return [(z * RING + y, (z + dz) % RING * RING + y) for z in range(RING) for y in range(RING)]


def spread(current):
    nq = current.shape[1]
    own = jnp.concatenate([current.astype(BF), jnp.ones((1, nq), BF), jnp.zeros((HALF - DIM - 1, nq), BF)], axis=0)
    return [own] + [lax.ppermute(own, "shk", shift(-j)) for j in range(1, RING)]


def per_device(savings, wealth, surplus, point_dims, point_levels, point_index, live_count, trans_counts):
    blocks = pack(surplus[0], point_dims, point_levels, point_index, live_count)
    groups = [
        [(2 * x + c) * 16 + z * RING + y for x in range(RING) for y in range(RING)] for c in range(2) for z in range(RING)
    ]
    mine = lax.all_to_all(blocks, ("pts", "shk"), 0, 0, tiled=True, axis_index_groups=groups)
    current = savings[0]
    income = wealth[0]
    queries = spread(current)
    mine, *queries = lax.optimization_barrier((mine, *queries))
    tables = (mine, lax.ppermute(mine, "pts", [(i, i ^ 1) for i in range(8)]))
    shock = lax.axis_index("shk")
    where = jnp.stack([shock // RING, shock % RING]).astype(jnp.int32)
    rowsum = jnp.sum(lax.dynamic_index_in_dim(trans_counts, shock, 0, keepdims=False))
    for sweep in range(ITERS):
        if sweep:
            queries = spread(current)
        parts = partial_sums(where, trans_counts, tables, queries)
        got = [parts[0]] + [lax.ppermute(parts[j], "shk", shift(j)) for j in range(1, RING)]
        if sweep == ITERS - 1:
            return finish(rowsum[None], current, jnp.transpose(wealth, (1, 0, 2)), got)
        expect = ((got[0] + got[1]) + (got[2] + got[3]))[:DIM] / rowsum.astype(F32)
        consumption = (BETA * expect) ** (-1.0 / GAMMA)
        current = (1.0 - damping) * current + damping * jax.nn.sigmoid(income - consumption)


def solution(mesh):
    return jax.shard_map(
        per_device,
        mesh=mesh,
        in_specs=(
            P("shk", None, "pts"),
            P("shk", None, "pts"),
            P("shk", None, "pts"),
            P("shk", None, "pts"),
            P("shk", None, "pts"),
            P("shk", None, "pts"),
            P("shk", "pts"),
            P(),
        ),
        out_specs=(P("shk", None, "pts"), P("shk", None, "pts")),
        check_vma=False,
    )
```

```python
import jax
import jax.numpy as jnp
from jax import lax
from jax.experimental import pallas as pl
from jax.experimental.pallas import tpu as pltpu
from jax.sharding import PartitionSpec as P

ITERS = 2
GAMMA = 2.0
BETA = 0.96
damping = 0.5
DIM = 59
HALF = 64
RING = 4
UNIT = 2
ROWS = 72
BF = jnp.bfloat16
F32 = jnp.float32
F8 = jnp.float8_e4m3fn
SPLIT = 32.0


def pack_kernel(live_ref, surplus_ref, dims_ref, levels_ref, index_ref, o_ref, wide_ref):
    npoints = surplus_ref.shape[1]
    position = lax.broadcasted_iota(jnp.int32, (1, npoints), 1)
    kept = position < live_ref[...]
    wide_ref[0 : 2 * DIM, :] = surplus_ref[...].astype(F32)
    exponent = wide_ref[DIM : 2 * DIM, :] - GAMMA * wide_ref[0:DIM, :]
    wide_ref[0:DIM, :] = jnp.where(kept, exponent, 0.0)
    row = lax.broadcasted_iota(jnp.int32, (16, npoints), 0) + (ROWS - 16)
    tail = jnp.where(row < DIM, wide_ref[ROWS - 16 : ROWS, :], 0.0)
    for k in range(3):
        level = levels_ref[k]
        refined = level > 0
        scale = jnp.where(refined, jnp.left_shift(jnp.ones_like(level), level), 0).astype(F32)
        bias = jnp.where(refined, 1 - index_ref[k], 1).astype(F32)
        for place, value in ((DIM + k, dims_ref[k].astype(F32)), (DIM + 3 + k, scale), (DIM + 6 + k, bias)):
            tail = jnp.where(row == place, value, tail)
    wide_ref[ROWS - 16 : ROWS, :] = tail
    block = wide_ref[0:ROWS, :].astype(BF)
    for g in range(o_ref.shape[0]):
        o_ref[g] = block


def pack(surplus, dims, levels, index, live):
    vm = pl.BlockSpec(memory_space=pltpu.VMEM)
    return pl.pallas_call(
        pack_kernel,
        out_shape=jax.ShapeDtypeStruct((16, ROWS, surplus.shape[1]), BF),
        in_specs=[vm] * 5,
        out_specs=vm,
        scratch_shapes=[pltpu.VMEM((120, surplus.shape[1]), F32)],
        name="pack_tables",
    )(live, surplus, *(jnp.transpose(v, (1, 0, 2)) for v in (dims, levels, index)))


def finish_kernel(rowsum_ref, now_ref, income_ref, g0, g1, g2, g3, cur_ref, con_ref):
    total = ((g0[...] + g1[...]) + (g2[...] + g3[...]))[:DIM]
    expect = total / rowsum_ref[0].astype(F32)
    consumption = (BETA * expect) ** (-1.0 / GAMMA)
    value = income_ref[:, 0, :] - consumption
    share = 1.0 / (1.0 + jnp.exp(-value))
    con_ref[:, 0, :] = consumption
    cur_ref[:, 0, :] = (1.0 - damping) * now_ref[...] + damping * share


def finish(rowsum, current, income, got):
    vm = pl.BlockSpec(memory_space=pltpu.VMEM)
    sm = pl.BlockSpec(memory_space=pltpu.SMEM)
    flat = jax.ShapeDtypeStruct((DIM, 1, current.shape[1]), F32)
    new, consumption = pl.pallas_call(
        finish_kernel,
        out_shape=[flat, flat],
        in_specs=[sm, vm, vm, vm, vm, vm, vm],
        out_specs=[vm, vm],
        compiler_params=pltpu.CompilerParams(vmem_limit_bytes=4 << 20),
        name="finish",
    )(rowsum, current, income, *got)
    return jnp.transpose(new, (1, 0, 2)), jnp.transpose(consumption, (1, 0, 2))


def kernel(
    where_ref, counts_ref, tab_a, tab_b, q0, q1, q2, q3, o0, o1, o2, o3, qt_ref, sel_a, sel_b, basis_a, basis_b, acc_ref
):
    z, y = where_ref[0], where_ref[1]
    for j, q in enumerate((q0, q1, q2, q3)):
        whole = q[...].astype(F32)
        whole = jnp.where(lax.broadcasted_iota(jnp.int32, whole.shape, 0) < DIM, whole * SPLIT, whole)
        high = whole.astype(F8).astype(F32)
        qt_ref[pl.ds(j * 128, 128), :] = jnp.concatenate([high, whole - high], axis=0).T.astype(F8)
    row = lax.broadcasted_iota(jnp.int32, (2 * HALF, 256), 0)
    coord = row % HALF
    units = 8 * RING // UNIT

    def block(u, b):
        return (tab_a, tab_b)[b][(u % RING) * RING + u // RING]

    def select(u, sel_ref):
        for b in range(UNIT):
            par = block(jnp.minimum(u, units - 1), b)[ROWS - 16 : ROWS].astype(F32)
            for k in range(3):
                dim = par[3 + k : 4 + k].astype(jnp.int32)
                scale = par[6 + k : 7 + k] * (1.0 / SPLIT)
                bias = par[9 + k : 10 + k]
                table = jnp.where(coord == dim, scale, jnp.where(row == DIM, bias, 0.0))
                sel_ref[b, k] = table.astype(F8)

    def hats(sel_ref, basis_ref):
        for b in range(UNIT):
            basis = None
            for k in range(3):
                left = jnp.dot(qt_ref[...], sel_ref[b, k], preferred_element_type=F32).astype(BF)
                factor = jnp.maximum(jnp.minimum(left, BF(2.0) - left), BF(0.0))
                basis = factor if basis is None else basis * factor
            basis_ref[:, pl.ds(b * 256, 256)] = basis

    def sums(u, basis_ref):
        weights = jnp.concatenate([block(u, b) for b in range(UNIT)], axis=1)
        acc_ref[u // RING] += lax.dot_general(
            basis_ref[...], weights, (((1,), (1,)), ((), ())), preferred_element_type=F32
        )

    acc_ref[...] = jnp.zeros_like(acc_ref)
    select(0, sel_a)
    select(1, sel_b)
    hats(sel_a, basis_a)
    select(2, sel_a)

    @pl.loop(0, units // 2 - 1)
    def _(it):
        u = 2 * it + 1
        hats(sel_b, basis_b)
        sums(u - 1, basis_a)
        select(u + 2, sel_b)
        hats(sel_a, basis_a)
        sums(u, basis_b)
        select(u + 3, sel_a)

    hats(sel_b, basis_b)
    sums(units - 2, basis_a)
    sums(units - 1, basis_b)

    for j, o in enumerate((o0, o1, o2, o3)):
        s = lax.rem(z + j, RING) * RING + y
        total = None
        for t in range(RING):
            value = acc_ref[t, pl.ds(j * 128, 128), :]
            count = counts_ref[s, z * RING + t].astype(F32)
            term = count * jnp.exp(value)
            total = term if total is None else total + term
        o[...] = total.T[:HALF]


def partial_sums(where, counts, tables, queries):
    vm = pl.BlockSpec(memory_space=pltpu.VMEM)
    sm = pl.BlockSpec(memory_space=pltpu.SMEM)
    return pl.pallas_call(
        kernel,
        out_shape=[jax.ShapeDtypeStruct((HALF, 128), F32)] * RING,
        in_specs=[sm, sm] + [vm] * 6,
        out_specs=[vm] * RING,
        scratch_shapes=[
            pltpu.VMEM((512, 2 * HALF), F8),
            pltpu.VMEM((UNIT, 3, 2 * HALF, 256), F8),
            pltpu.VMEM((UNIT, 3, 2 * HALF, 256), F8),
            pltpu.VMEM((512, UNIT * 256), BF),
            pltpu.VMEM((512, UNIT * 256), BF),
            pltpu.VMEM((RING, 512, ROWS), F32),
        ],
        compiler_params=pltpu.CompilerParams(vmem_limit_bytes=40 << 20),
        name="euler_basis",
    )(where, counts, *tables, *queries)


def shift(dz):
    return [(z * RING + y, (z + dz) % RING * RING + y) for z in range(RING) for y in range(RING)]


def spread(current):
    nq = current.shape[1]
    own = jnp.concatenate([current.astype(BF), jnp.ones((1, nq), BF), jnp.zeros((HALF - DIM - 1, nq), BF)], axis=0)
    return [own] + [lax.ppermute(own, "shk", shift(-j)) for j in range(1, RING)]


def per_device(savings, wealth, surplus, point_dims, point_levels, point_index, live_count, trans_counts):
    blocks = pack(surplus[0], point_dims, point_levels, point_index, live_count)
    groups = [
        [(2 * x + c) * 16 + z * RING + y for x in range(RING) for y in range(RING)] for c in range(2) for z in range(RING)
    ]
    mine = lax.all_to_all(blocks, ("pts", "shk"), 0, 0, tiled=True, axis_index_groups=groups)
    current = savings[0]
    income = wealth[0]
    queries = spread(current)
    mine, *queries = lax.optimization_barrier((mine, *queries))
    tables = (mine, lax.ppermute(mine, "pts", [(i, i ^ 1) for i in range(8)]))
    shock = lax.axis_index("shk")
    where = jnp.stack([shock // RING, shock % RING]).astype(jnp.int32)
    rowsum = jnp.sum(lax.dynamic_index_in_dim(trans_counts, shock, 0, keepdims=False))
    for sweep in range(ITERS):
        if sweep:
            queries = spread(current)
        parts = partial_sums(where, trans_counts, tables, queries)
        got = [parts[0]] + [lax.ppermute(parts[j], "shk", shift(j)) for j in range(1, RING)]
        if sweep == ITERS - 1:
            return finish(rowsum[None], current, jnp.transpose(wealth, (1, 0, 2)), got)
        expect = ((got[0] + got[1]) + (got[2] + got[3]))[:DIM] / rowsum.astype(F32)
        consumption = (BETA * expect) ** (-1.0 / GAMMA)
        current = (1.0 - damping) * current + damping * jax.nn.sigmoid(income - consumption)


def solution(mesh):
    return jax.shard_map(
        per_device,
        mesh=mesh,
        in_specs=(
            P("shk", None, "pts"),
            P("shk", None, "pts"),
            P("shk", None, "pts"),
            P("shk", None, "pts"),
            P("shk", None, "pts"),
            P("shk", None, "pts"),
            P("shk", "pts"),
            P(),
        ),
        out_specs=(P("shk", None, "pts"), P("shk", None, "pts")),
        check_vma=False,
    )
```

```python
import jax
import jax.numpy as jnp
from jax import lax
from jax.experimental import pallas as pl
from jax.experimental.pallas import tpu as pltpu
from jax.sharding import PartitionSpec as P

ITERS = 2
GAMMA = 2.0
BETA = 0.96
damping = 0.5
DIM = 59
HALF = 64
RING = 4
UNIT = 2
ROWS = 72
STEP = 0.375 / 32768
BF = jnp.bfloat16
F32 = jnp.float32
F8 = jnp.float8_e4m3fn
SPLIT = 32.0


def pack_kernel(live_ref, surplus_ref, dims_ref, levels_ref, index_ref, o_ref, wide_ref):
    npoints = surplus_ref.shape[1]
    position = lax.broadcasted_iota(jnp.int32, (1, npoints), 1)
    kept = position < live_ref[...]
    wide_ref[0 : 2 * DIM, :] = surplus_ref[...].astype(F32)
    exponent = wide_ref[DIM : 2 * DIM, :] - GAMMA * wide_ref[0:DIM, :]
    steps = jnp.clip(jnp.floor(exponent * (1.0 / STEP) + 0.5), -32767.0, 32767.0)
    wide_ref[0:DIM, :] = jnp.where(kept, steps, 0.0)
    row = lax.broadcasted_iota(jnp.int32, (16, npoints), 0) + (ROWS - 16)
    tail = jnp.where(row < DIM, wide_ref[ROWS - 16 : ROWS, :], 0.0)
    for k in range(3):
        level = levels_ref[k]
        refined = level > 0
        scale = jnp.where(refined, jnp.left_shift(jnp.ones_like(level), level), 0).astype(F32)
        bias = jnp.where(refined, 1 - index_ref[k], 1).astype(F32)
        for place, value in ((DIM + k, dims_ref[k].astype(F32)), (DIM + 3 + k, scale), (DIM + 6 + k, bias)):
            tail = jnp.where(row == place, value, tail)
    wide_ref[ROWS - 16 : ROWS, :] = tail
    block = wide_ref[0:ROWS, :].astype(jnp.int32).astype(jnp.int16)
    for g in range(o_ref.shape[0]):
        o_ref[g] = block


def pack(surplus, dims, levels, index, live):
    vm = pl.BlockSpec(memory_space=pltpu.VMEM)
    return pl.pallas_call(
        pack_kernel,
        out_shape=jax.ShapeDtypeStruct((16, ROWS, surplus.shape[1]), jnp.int16),
        in_specs=[vm] * 5,
        out_specs=vm,
        scratch_shapes=[pltpu.VMEM((120, surplus.shape[1]), F32)],
        name="pack_tables",
    )(live, surplus, *(jnp.transpose(v, (1, 0, 2)) for v in (dims, levels, index)))


def finish_kernel(rowsum_ref, now_ref, income_ref, g0, g1, g2, g3, cur_ref, con_ref):
    total = ((g0[...] + g1[...]) + (g2[...] + g3[...]))[:DIM]
    expect = total / rowsum_ref[0].astype(F32)
    consumption = (BETA * expect) ** (-1.0 / GAMMA)
    value = income_ref[:, 0, :] - consumption
    share = 1.0 / (1.0 + jnp.exp(-value))
    con_ref[:, 0, :] = consumption
    cur_ref[:, 0, :] = (1.0 - damping) * now_ref[...] + damping * share


def finish(rowsum, current, income, got):
    vm = pl.BlockSpec(memory_space=pltpu.VMEM)
    sm = pl.BlockSpec(memory_space=pltpu.SMEM)
    flat = jax.ShapeDtypeStruct((DIM, 1, current.shape[1]), F32)
    new, consumption = pl.pallas_call(
        finish_kernel,
        out_shape=[flat, flat],
        in_specs=[sm, vm, vm, vm, vm, vm, vm],
        out_specs=[vm, vm],
        compiler_params=pltpu.CompilerParams(vmem_limit_bytes=4 << 20),
        name="finish",
    )(rowsum, current, income, *got)
    return jnp.transpose(new, (1, 0, 2)), jnp.transpose(consumption, (1, 0, 2))


def kernel(
    where_ref, counts_ref, tab_a, tab_b, q0, q1, q2, q3, o0, o1, o2, o3, qt_ref, sel_a, sel_b, basis_a, basis_b, acc_ref
):
    z, y = where_ref[0], where_ref[1]
    for j, q in enumerate((q0, q1, q2, q3)):
        whole = q[...].astype(F32)
        whole = jnp.where(lax.broadcasted_iota(jnp.int32, whole.shape, 0) < DIM, whole * SPLIT, whole)
        high = whole.astype(F8).astype(F32)
        qt_ref[pl.ds(j * 128, 128), :] = jnp.concatenate([high, whole - high], axis=0).T.astype(F8)
    row = lax.broadcasted_iota(jnp.int32, (HALF, 256), 0)
    units = 8 * RING // UNIT

    def block(u, b):
        return (tab_a, tab_b)[b][(u % RING) * RING + u // RING]

    def select(u, sel_ref):
        for b in range(UNIT):
            par = block(jnp.minimum(u, units - 1), b)[ROWS - 16 : ROWS].astype(jnp.int32)
            for k in range(3):
                dim = par[3 + k : 4 + k]
                scale = par[6 + k : 7 + k].astype(F32) * (1.0 / SPLIT)
                bias = par[9 + k : 10 + k].astype(F32)
                table = jnp.where(row == dim, scale, jnp.where(row == DIM, bias, 0.0)).astype(F8)
                sel_ref[b, k, 0:HALF, :] = table
                sel_ref[b, k, HALF : 2 * HALF, :] = table

    def hats(sel_ref, basis_ref):
        for b in range(UNIT):
            basis = None
            for k in range(3):
                left = jnp.dot(qt_ref[...], sel_ref[b, k], preferred_element_type=F32)
                factor = jnp.minimum(left, 2.0 - left)
                factor = jnp.maximum(factor, 0.0) if k < 2 else factor
                basis = factor if basis is None else basis * factor
            basis_ref[:, pl.ds(b * 256, 256)] = jnp.maximum(basis.astype(BF), BF(0.0))

    def halves(blk):
        steps = blk[0:HALF].astype(jnp.int32)
        high = jnp.right_shift(steps, 8)
        return jnp.concatenate([high.astype(F32), (steps - high * 256).astype(F32)], axis=0).astype(BF)

    def sums(u, basis_ref):
        weights = jnp.concatenate([halves(block(u, b)) for b in range(UNIT)], axis=1)
        acc_ref[u // RING] += lax.dot_general(
            basis_ref[...], weights, (((1,), (1,)), ((), ())), preferred_element_type=F32
        )

    acc_ref[...] = jnp.zeros_like(acc_ref)
    select(0, sel_a)
    select(1, sel_b)
    hats(sel_a, basis_a)
    select(2, sel_a)

    @pl.loop(0, units // 2 - 1)
    def _(it):
        u = 2 * it + 1
        hats(sel_b, basis_b)
        sums(u - 1, basis_a)
        select(u + 2, sel_b)
        hats(sel_a, basis_a)
        sums(u, basis_b)
        select(u + 3, sel_a)

    hats(sel_b, basis_b)
    sums(units - 2, basis_a)
    sums(units - 1, basis_b)

    for j, o in enumerate((o0, o1, o2, o3)):
        s = lax.rem(z + j, RING) * RING + y
        total = None
        for t in range(RING):
            value = acc_ref[t, pl.ds(j * 128, 128), :]
            count = counts_ref[s, z * RING + t].astype(F32)
            term = count * jnp.exp((256.0 * STEP) * value + STEP * pltpu.roll(value, HALF, 1))
            total = term if total is None else total + term
        o[...] = total.T[:HALF]


def partial_sums(where, counts, tables, queries):
    vm = pl.BlockSpec(memory_space=pltpu.VMEM)
    sm = pl.BlockSpec(memory_space=pltpu.SMEM)
    return pl.pallas_call(
        kernel,
        out_shape=[jax.ShapeDtypeStruct((HALF, 128), F32)] * RING,
        in_specs=[sm, sm] + [vm] * 6,
        out_specs=[vm] * RING,
        scratch_shapes=[
            pltpu.VMEM((512, 2 * HALF), F8),
            pltpu.VMEM((UNIT, 3, 2 * HALF, 256), F8),
            pltpu.VMEM((UNIT, 3, 2 * HALF, 256), F8),
            pltpu.VMEM((512, UNIT * 256), BF),
            pltpu.VMEM((512, UNIT * 256), BF),
            pltpu.VMEM((RING, 512, 128), F32),
        ],
        compiler_params=pltpu.CompilerParams(vmem_limit_bytes=40 << 20),
        name="euler_basis",
    )(where, counts, *tables, *queries)


def shift(dz):
    return [(z * RING + y, (z + dz) % RING * RING + y) for z in range(RING) for y in range(RING)]


def spread(current):
    nq = current.shape[1]
    own = jnp.concatenate([current.astype(BF), jnp.ones((1, nq), BF), jnp.zeros((HALF - DIM - 1, nq), BF)], axis=0)
    return [own] + [lax.ppermute(own, "shk", shift(-j)) for j in range(1, RING)]


def per_device(savings, wealth, surplus, point_dims, point_levels, point_index, live_count, trans_counts):
    blocks = pack(surplus[0], point_dims, point_levels, point_index, live_count)
    groups = [
        [(2 * x + c) * 16 + z * RING + y for x in range(RING) for y in range(RING)] for c in range(2) for z in range(RING)
    ]
    mine = lax.all_to_all(blocks, ("pts", "shk"), 0, 0, tiled=True, axis_index_groups=groups)
    current = savings[0]
    income = wealth[0]
    queries = spread(current)
    mine, *queries = lax.optimization_barrier((mine, *queries))
    tables = (mine, lax.ppermute(mine, "pts", [(i, i ^ 1) for i in range(8)]))
    shock = lax.axis_index("shk")
    where = jnp.stack([shock // RING, shock % RING]).astype(jnp.int32)
    rowsum = jnp.sum(lax.dynamic_index_in_dim(trans_counts, shock, 0, keepdims=False))
    for sweep in range(ITERS):
        if sweep:
            queries = spread(current)
        parts = partial_sums(where, trans_counts, tables, queries)
        got = [parts[0]] + [lax.ppermute(parts[j], "shk", shift(j)) for j in range(1, RING)]
        if sweep == ITERS - 1:
            return finish(rowsum[None], current, jnp.transpose(wealth, (1, 0, 2)), got)
        expect = ((got[0] + got[1]) + (got[2] + got[3]))[:DIM] / rowsum.astype(F32)
        consumption = (BETA * expect) ** (-1.0 / GAMMA)
        current = (1.0 - damping) * current + damping * jax.nn.sigmoid(income - consumption)


def solution(mesh):
    return jax.shard_map(
        per_device,
        mesh=mesh,
        in_specs=(
            P("shk", None, "pts"),
            P("shk", None, "pts"),
            P("shk", None, "pts"),
            P("shk", None, "pts"),
            P("shk", None, "pts"),
            P("shk", None, "pts"),
            P("shk", "pts"),
            P(),
        ),
        out_specs=(P("shk", None, "pts"), P("shk", None, "pts")),
        check_vma=False,
    )
```

```python
import functools

import jax
import jax.numpy as jnp
from jax import lax
from jax.experimental import pallas as pl
from jax.experimental.pallas import tpu as pltpu
from jax.sharding import PartitionSpec as P

GAMMA = 2.0
BETA = 0.96
damping = 0.5
DIM = 59
HALF = 64
RING = 4
UNIT = 2
ROWS = 72
STEP = 0.375 / 32768
BF = jnp.bfloat16
F32 = jnp.float32
F8 = jnp.float8_e4m3fn
SPLIT = 32.0


def pack_kernel(live_ref, surplus_ref, dims_ref, levels_ref, index_ref, o_ref, wide_ref):
    npoints = surplus_ref.shape[1]
    position = lax.broadcasted_iota(jnp.int32, (1, npoints), 1)
    kept = position < live_ref[...]
    wide_ref[0 : 2 * DIM, :] = surplus_ref[...].astype(F32)
    exponent = wide_ref[DIM : 2 * DIM, :] - GAMMA * wide_ref[0:DIM, :]
    steps = jnp.clip(jnp.floor(exponent * (1.0 / STEP) + 0.5), -32767.0, 32767.0)
    wide_ref[0:DIM, :] = jnp.where(kept, steps, 0.0)
    row = lax.broadcasted_iota(jnp.int32, (16, npoints), 0) + (ROWS - 16)
    tail = jnp.where(row < DIM, wide_ref[ROWS - 16 : ROWS, :], 0.0)
    for k in range(3):
        level = levels_ref[k]
        refined = level > 0
        scale = jnp.where(refined, jnp.left_shift(jnp.ones_like(level), level), 0).astype(F32)
        bias = jnp.where(refined, 1 - index_ref[k], 1).astype(F32)
        for place, value in ((DIM + k, dims_ref[k].astype(F32)), (DIM + 3 + k, scale), (DIM + 6 + k, bias)):
            tail = jnp.where(row == place, value, tail)
    wide_ref[ROWS - 16 : ROWS, :] = tail
    block = wide_ref[0:ROWS, :].astype(jnp.int32).astype(jnp.int16)
    for g in range(o_ref.shape[0]):
        o_ref[g] = block


def pack(surplus, dims, levels, index, live):
    vm = pl.BlockSpec(memory_space=pltpu.VMEM)
    return pl.pallas_call(
        pack_kernel,
        out_shape=jax.ShapeDtypeStruct((16, ROWS, surplus.shape[1]), jnp.int16),
        in_specs=[vm] * 5,
        out_specs=vm,
        scratch_shapes=[pltpu.VMEM((120, surplus.shape[1]), F32)],
        name="pack_tables",
    )(live, surplus, *(jnp.transpose(v, (1, 0, 2)) for v in (dims, levels, index)))


def advance_kernel(where_ref, counts_ref, p0, p1, p2, p3, s0, s1, s2, s3, q0, q1, q2, q3, cur_ref):
    z, y = where_ref[0], where_ref[1]
    row = lax.broadcasted_iota(jnp.int32, (HALF, 128), 0)
    for j, (state, q) in enumerate(((s0, q0), (s1, q1), (s2, q2), (s3, q3))):
        s = lax.rem(z + j, RING) * RING + y
        rowsum = counts_ref[s, 0]
        for t in range(1, RING * RING):
            rowsum += counts_ref[s, t]
        total = (p0[j] + p2[(j - 2) % RING]) + (p1[(j - 1) % RING] + p3[(j - 3) % RING])
        consumption = (BETA * (total / rowsum.astype(F32))) ** (-1.0 / GAMMA)
        share = 1.0 / (1.0 + jnp.exp(consumption - state[1]))
        new = (1.0 - damping) * state[0] + damping * share
        new = jnp.where(row < DIM, new, jnp.where(row == DIM, 1.0, 0.0))
        q[...] = new.astype(BF)
        if j == 0:
            cur_ref[...] = new


def advance(where, counts, parts, states):
    vm = pl.BlockSpec(memory_space=pltpu.VMEM)
    sm = pl.BlockSpec(memory_space=pltpu.SMEM)
    *queries, current = pl.pallas_call(
        advance_kernel,
        out_shape=[jax.ShapeDtypeStruct((HALF, 128), BF)] * RING + [jax.ShapeDtypeStruct((HALF, 128), F32)],
        in_specs=[sm, sm] + [vm] * (2 * RING),
        out_specs=[vm] * (RING + 1),
        compiler_params=pltpu.CompilerParams(vmem_limit_bytes=4 << 20),
        name="advance",
    )(where, counts, *parts, *states)
    return queries, current


def finish_kernel(rowsum_ref, now_ref, income_ref, g0, g1, g2, g3, cur_ref, con_ref):
    total = ((g0[...] + g1[...]) + (g2[...] + g3[...]))[:DIM]
    expect = total / rowsum_ref[0].astype(F32)
    consumption = (BETA * expect) ** (-1.0 / GAMMA)
    value = income_ref[:, 0, :] - consumption
    share = 1.0 / (1.0 + jnp.exp(-value))
    con_ref[:, 0, :] = consumption
    cur_ref[:, 0, :] = (1.0 - damping) * now_ref[0:DIM, :] + damping * share


def finish(rowsum, current, income, got):
    vm = pl.BlockSpec(memory_space=pltpu.VMEM)
    sm = pl.BlockSpec(memory_space=pltpu.SMEM)
    flat = jax.ShapeDtypeStruct((DIM, 1, current.shape[1]), F32)
    new, consumption = pl.pallas_call(
        finish_kernel,
        out_shape=[flat, flat],
        in_specs=[sm, vm, vm, vm, vm, vm, vm],
        out_specs=[vm, vm],
        compiler_params=pltpu.CompilerParams(vmem_limit_bytes=4 << 20),
        name="finish",
    )(rowsum, current, income, *got)
    return jnp.transpose(new, (1, 0, 2)), jnp.transpose(consumption, (1, 0, 2))


def kernel(
    first, where_ref, counts_ref, tab_a, tab_b, q0, q1, q2, q3, *refs
):
    outs, (qt_ref, sel_a, sel_b, basis_a, basis_b, acc_ref) = refs[:-6], refs[-6:]
    z, y = where_ref[0], where_ref[1]
    for j, q in enumerate((q0, q1, q2, q3)):
        whole = (q[0] if first else q[...]).astype(BF).astype(F32)
        whole = jnp.where(lax.broadcasted_iota(jnp.int32, whole.shape, 0) < DIM, whole * SPLIT, whole)
        high = whole.astype(F8).astype(F32)
        qt_ref[pl.ds(j * 128, 128), :] = jnp.concatenate([high, whole - high], axis=0).T.astype(F8)
    row = lax.broadcasted_iota(jnp.int32, (HALF, 256), 0)
    units = 8 * RING // UNIT

    def block(u, b):
        return (tab_a, tab_b)[b][(u % RING) * RING + u // RING]

    def select(u, sel_ref):
        for b in range(UNIT):
            par = block(jnp.minimum(u, units - 1), b)[ROWS - 16 : ROWS].astype(jnp.int32)
            for k in range(3):
                dim = par[3 + k : 4 + k]
                scale = par[6 + k : 7 + k].astype(F32) * (1.0 / SPLIT)
                bias = par[9 + k : 10 + k].astype(F32)
                table = jnp.where(row == dim, scale, jnp.where(row == DIM, bias, 0.0)).astype(F8)
                sel_ref[b, k, 0:HALF, :] = table
                sel_ref[b, k, HALF : 2 * HALF, :] = table

    def hats(sel_ref, basis_ref):
        for b in range(UNIT):
            basis = None
            for k in range(3):
                left = jnp.dot(qt_ref[...], sel_ref[b, k], preferred_element_type=F32)
                factor = jnp.minimum(left, 2.0 - left)
                factor = jnp.maximum(factor, 0.0) if k < 2 else factor
                basis = factor if basis is None else basis * factor
            basis_ref[:, pl.ds(b * 256, 256)] = jnp.maximum(basis.astype(BF), BF(0.0))

    def halves(blk):
        steps = blk[0:HALF].astype(jnp.int32).astype(F32)
        high = steps.astype(BF)
        return jnp.concatenate([high, (steps - high.astype(F32)).astype(BF)], axis=0)

    def sums(u, basis_ref):
        weights = jnp.concatenate([halves(block(u, b)) for b in range(UNIT)], axis=1)
        acc_ref[u // RING] += lax.dot_general(
            basis_ref[...], weights, (((1,), (1,)), ((), ())), preferred_element_type=F32
        )

    acc_ref[...] = jnp.zeros_like(acc_ref)
    select(0, sel_a)
    select(1, sel_b)
    hats(sel_a, basis_a)
    select(2, sel_a)

    @pl.loop(0, units // 2 - 1)
    def _(it):
        u = 2 * it + 1
        hats(sel_b, basis_b)
        sums(u - 1, basis_a)
        select(u + 2, sel_b)
        hats(sel_a, basis_a)
        sums(u, basis_b)
        select(u + 3, sel_a)

    hats(sel_b, basis_b)
    sums(units - 2, basis_a)
    sums(units - 1, basis_b)

    for j in range(RING):
        s = lax.rem(z + j, RING) * RING + y
        total = None
        for t in range(RING):
            value = acc_ref[t, pl.ds(j * 128, 128), :]
            count = counts_ref[s, z * RING + t].astype(F32)
            term = count * jnp.exp(STEP * (value + pltpu.roll(value, HALF, 1)))
            total = term if total is None else total + term
        if first:
            outs[0][j] = total.T[:HALF]
        else:
            outs[j][...] = total.T[:HALF]


def partial_sums(first, where, counts, tables, queries):
    vm = pl.BlockSpec(memory_space=pltpu.VMEM)
    sm = pl.BlockSpec(memory_space=pltpu.SMEM)
    if first:
        shapes = [jax.ShapeDtypeStruct((RING, HALF, 128), F32)]
    else:
        shapes = [jax.ShapeDtypeStruct((HALF, 128), F32)] * RING
    return pl.pallas_call(
        functools.partial(kernel, first),
        out_shape=shapes,
        in_specs=[sm, sm] + [vm] * 6,
        out_specs=[vm] * len(shapes),
        scratch_shapes=[
            pltpu.VMEM((512, 2 * HALF), F8),
            pltpu.VMEM((UNIT, 3, 2 * HALF, 256), F8),
            pltpu.VMEM((UNIT, 3, 2 * HALF, 256), F8),
            pltpu.VMEM((512, UNIT * 256), BF),
            pltpu.VMEM((512, UNIT * 256), BF),
            pltpu.VMEM((RING, 512, 128), F32),
        ],
        compiler_params=pltpu.CompilerParams(vmem_limit_bytes=40 << 20),
        name="euler_basis",
    )(where, counts, *tables, *queries)


def shift(dz):
    return [(z * RING + y, (z + dz) % RING * RING + y) for z in range(RING) for y in range(RING)]


def spread(current, income):
    nq = current.shape[1]
    rest = jnp.zeros((HALF - DIM - 1, nq), F32)
    one = jnp.ones((1, nq), F32)
    own = jnp.stack([jnp.concatenate([v, one, rest], axis=0) for v in (current, income)])
    return [own] + [lax.ppermute(own, "shk", shift(-j)) for j in range(1, RING)]


def per_device(savings, wealth, surplus, point_dims, point_levels, point_index, live_count, trans_counts):
    blocks = pack(surplus[0], point_dims, point_levels, point_index, live_count)
    groups = [
        [(2 * x + c) * 16 + z * RING + y for x in range(RING) for y in range(RING)] for c in range(2) for z in range(RING)
    ]
    mine = lax.all_to_all(blocks, ("pts", "shk"), 0, 0, tiled=True, axis_index_groups=groups)
    states = spread(savings[0], wealth[0])
    mine, *states = lax.optimization_barrier((mine, *states))
    tables = (mine, lax.ppermute(mine, "pts", [(i, i ^ 1) for i in range(8)]))
    shock = lax.axis_index("shk")
    where = jnp.stack([shock // RING, shock % RING]).astype(jnp.int32)
    rowsum = jnp.sum(lax.dynamic_index_in_dim(trans_counts, shock, 0, keepdims=False))
    (sums,) = partial_sums(True, where, trans_counts, tables, states)
    parts = [sums] + [lax.ppermute(sums, "shk", shift(-k)) for k in range(1, RING)]
    queries, current = advance(where, trans_counts, parts, states)
    parts = partial_sums(False, where, trans_counts, tables, queries)
    got = [parts[0]] + [lax.ppermute(parts[j], "shk", shift(j)) for j in range(1, RING)]
    return finish(rowsum[None], current, jnp.transpose(wealth, (1, 0, 2)), got)


def solution(mesh):
    return jax.shard_map(
        per_device,
        mesh=mesh,
        in_specs=(
            P("shk", None, "pts"),
            P("shk", None, "pts"),
            P("shk", None, "pts"),
            P("shk", None, "pts"),
            P("shk", None, "pts"),
            P("shk", None, "pts"),
            P("shk", "pts"),
            P(),
        ),
        out_specs=(P("shk", None, "pts"), P("shk", None, "pts")),
        check_vma=False,
    )
```

```python
import functools

import jax
import jax.numpy as jnp
from jax import lax
from jax.experimental import pallas as pl
from jax.experimental.pallas import tpu as pltpu
from jax.sharding import PartitionSpec as P

GAMMA = 2.0
BETA = 0.96
damping = 0.5
DIM = 59
HALF = 64
RING = 4
UNIT = 2
ROWS = 72
STEP = 0.375 / 32768
BF = jnp.bfloat16
F32 = jnp.float32
F8 = jnp.float8_e4m3fn
SPLIT = 32.0


def pack_kernel(live_ref, surplus_ref, dims_ref, levels_ref, index_ref, o_ref, wide_ref):
    npoints = surplus_ref.shape[1]
    position = lax.broadcasted_iota(jnp.int32, (1, npoints), 1)
    kept = position < live_ref[...]
    wide_ref[0 : 2 * DIM, :] = surplus_ref[...].astype(F32)
    exponent = wide_ref[DIM : 2 * DIM, :] - GAMMA * wide_ref[0:DIM, :]
    steps = jnp.clip(jnp.floor(exponent * (1.0 / STEP) + 0.5), -32767.0, 32767.0)
    wide_ref[0:DIM, :] = jnp.where(kept, steps, 0.0)
    row = lax.broadcasted_iota(jnp.int32, (16, npoints), 0) + (ROWS - 16)
    tail = jnp.where(row < DIM, wide_ref[ROWS - 16 : ROWS, :], 0.0)
    for k in range(3):
        level = levels_ref[k]
        refined = level > 0
        scale = jnp.where(refined, jnp.left_shift(jnp.ones_like(level), level), 0).astype(F32)
        bias = jnp.where(refined, 1 - index_ref[k], 1).astype(F32)
        for place, value in ((DIM + k, dims_ref[k].astype(F32)), (DIM + 3 + k, scale), (DIM + 6 + k, bias)):
            tail = jnp.where(row == place, value, tail)
    wide_ref[ROWS - 16 : ROWS, :] = tail
    block = wide_ref[0:ROWS, :].astype(jnp.int32).astype(jnp.int16)
    for g in range(o_ref.shape[0]):
        o_ref[g] = block


def pack(surplus, dims, levels, index, live):
    vm = pl.BlockSpec(memory_space=pltpu.VMEM)
    return pl.pallas_call(
        pack_kernel,
        out_shape=jax.ShapeDtypeStruct((16, ROWS, surplus.shape[1]), jnp.int16),
        in_specs=[vm] * 5,
        out_specs=vm,
        scratch_shapes=[pltpu.VMEM((120, surplus.shape[1]), F32)],
        name="pack_tables",
    )(live, surplus, *(jnp.transpose(v, (1, 0, 2)) for v in (dims, levels, index)))


def advance_kernel(where_ref, counts_ref, p0, p1, p2, p3, s0, s1, s2, s3, q0, q1, q2, q3, cur_ref):
    z, y = where_ref[0], where_ref[1]
    row = lax.broadcasted_iota(jnp.int32, (HALF, 128), 0)
    for j, (state, q) in enumerate(((s0, q0), (s1, q1), (s2, q2), (s3, q3))):
        s = lax.rem(z + j, RING) * RING + y
        rowsum = counts_ref[s, 0]
        for t in range(1, RING * RING):
            rowsum += counts_ref[s, t]
        total = (p0[j] + p2[(j - 2) % RING]) + (p1[(j - 1) % RING] + p3[(j - 3) % RING])
        consumption = (BETA * (total / rowsum.astype(F32))) ** (-1.0 / GAMMA)
        share = 1.0 / (1.0 + jnp.exp(consumption - state[1]))
        new = (1.0 - damping) * state[0] + damping * share
        new = jnp.where(row < DIM, new, jnp.where(row == DIM, 1.0, 0.0))
        q[...] = new.astype(BF)
        if j == 0:
            cur_ref[...] = new


def advance(where, counts, parts, states):
    vm = pl.BlockSpec(memory_space=pltpu.VMEM)
    sm = pl.BlockSpec(memory_space=pltpu.SMEM)
    *queries, current = pl.pallas_call(
        advance_kernel,
        out_shape=[jax.ShapeDtypeStruct((HALF, 128), BF)] * RING + [jax.ShapeDtypeStruct((HALF, 128), F32)],
        in_specs=[sm, sm] + [vm] * (2 * RING),
        out_specs=[vm] * (RING + 1),
        compiler_params=pltpu.CompilerParams(vmem_limit_bytes=4 << 20),
        name="advance",
    )(where, counts, *parts, *states)
    return queries, current


def finish_kernel(where_ref, counts_ref, now_ref, income_ref, g0, g1, g2, g3, cur_ref, con_ref):
    total = ((g0[...] + g1[...]) + (g2[...] + g3[...]))[:DIM]
    s = where_ref[0] * RING + where_ref[1]
    rowsum = counts_ref[s, 0]
    for t in range(1, RING * RING):
        rowsum += counts_ref[s, t]
    expect = total / rowsum.astype(F32)
    consumption = (BETA * expect) ** (-1.0 / GAMMA)
    value = income_ref[:, 0, :] - consumption
    share = 1.0 / (1.0 + jnp.exp(-value))
    con_ref[:, 0, :] = consumption
    cur_ref[:, 0, :] = (1.0 - damping) * now_ref[0:DIM, :] + damping * share


def finish(where, counts, current, income, got):
    vm = pl.BlockSpec(memory_space=pltpu.VMEM)
    sm = pl.BlockSpec(memory_space=pltpu.SMEM)
    flat = jax.ShapeDtypeStruct((DIM, 1, current.shape[1]), F32)
    new, consumption = pl.pallas_call(
        finish_kernel,
        out_shape=[flat, flat],
        in_specs=[sm, sm] + [vm] * 6,
        out_specs=[vm, vm],
        compiler_params=pltpu.CompilerParams(vmem_limit_bytes=4 << 20),
        name="finish",
    )(where, counts, current, income, *got)
    return jnp.transpose(new, (1, 0, 2)), jnp.transpose(consumption, (1, 0, 2))


def kernel(
    first, where_ref, counts_ref, tab_a, tab_b, q0, q1, q2, q3, *refs
):
    outs, (qt_ref, sel_a, sel_b, basis_a, basis_b, acc_ref) = refs[:-6], refs[-6:]
    z, y = where_ref[0], where_ref[1]
    for j, q in enumerate((q0, q1, q2, q3)):
        whole = (q[0] if first else q[...]).astype(BF).astype(F32)
        whole = jnp.where(lax.broadcasted_iota(jnp.int32, whole.shape, 0) < DIM, whole * SPLIT, whole)
        high = whole.astype(F8).astype(F32)
        qt_ref[pl.ds(j * 128, 128), :] = jnp.concatenate([high, whole - high], axis=0).T.astype(F8)
    row = lax.broadcasted_iota(jnp.int32, (HALF, 256), 0)
    units = 8 * RING // UNIT

    def block(u, b):
        return (tab_a, tab_b)[b][(u % RING) * RING + u // RING]

    def select(u, sel_ref):
        for b in range(UNIT):
            par = block(jnp.minimum(u, units - 1), b)[ROWS - 16 : ROWS].astype(jnp.int32)
            for k in range(3):
                dim = par[3 + k : 4 + k]
                scale = par[6 + k : 7 + k].astype(F32) * (1.0 / SPLIT)
                bias = par[9 + k : 10 + k].astype(F32)
                table = jnp.where(row == dim, scale, jnp.where(row == DIM, bias, 0.0)).astype(F8)
                sel_ref[b, k, 0:HALF, :] = table
                sel_ref[b, k, HALF : 2 * HALF, :] = table

    def hats(sel_ref, basis_ref):
        for b in range(UNIT):
            basis = None
            for k in range(3):
                left = jnp.dot(qt_ref[...], sel_ref[b, k], preferred_element_type=F32)
                factor = jnp.minimum(left, 2.0 - left)
                factor = jnp.maximum(factor, 0.0) if k < 2 else factor
                basis = factor if basis is None else basis * factor
            basis_ref[:, pl.ds(b * 256, 256)] = jnp.maximum(basis.astype(BF), BF(0.0))

    def halves(blk):
        steps = blk[0:HALF].astype(jnp.int32).astype(F32)
        high = steps.astype(BF)
        return jnp.concatenate([high, (steps - high.astype(F32)).astype(BF)], axis=0)

    def sums(u, basis_ref):
        weights = jnp.concatenate([halves(block(u, b)) for b in range(UNIT)], axis=1)
        acc_ref[u // RING] += lax.dot_general(
            basis_ref[...], weights, (((1,), (1,)), ((), ())), preferred_element_type=F32
        )

    acc_ref[...] = jnp.zeros_like(acc_ref)
    select(0, sel_a)
    select(1, sel_b)
    hats(sel_a, basis_a)
    select(2, sel_a)

    @pl.loop(0, units // 2 - 1)
    def _(it):
        u = 2 * it + 1
        hats(sel_b, basis_b)
        sums(u - 1, basis_a)
        select(u + 2, sel_b)
        hats(sel_a, basis_a)
        sums(u, basis_b)
        select(u + 3, sel_a)

    hats(sel_b, basis_b)
    sums(units - 2, basis_a)
    sums(units - 1, basis_b)

    for j in range(RING):
        s = lax.rem(z + j, RING) * RING + y
        total = None
        for t in range(RING):
            value = acc_ref[t, pl.ds(j * 128, 128), :]
            count = counts_ref[s, z * RING + t].astype(F32)
            term = count * jnp.exp(STEP * (value + pltpu.roll(value, HALF, 1)))
            total = term if total is None else total + term
        if first:
            outs[0][j] = total.T[:HALF]
        else:
            outs[j][...] = total.T[:HALF]


def partial_sums(first, where, counts, tables, queries):
    vm = pl.BlockSpec(memory_space=pltpu.VMEM)
    sm = pl.BlockSpec(memory_space=pltpu.SMEM)
    if first:
        shapes = [jax.ShapeDtypeStruct((RING, HALF, 128), F32)]
    else:
        shapes = [jax.ShapeDtypeStruct((HALF, 128), F32)] * RING
    return pl.pallas_call(
        functools.partial(kernel, first),
        out_shape=shapes,
        in_specs=[sm, sm] + [vm] * 6,
        out_specs=[vm] * len(shapes),
        scratch_shapes=[
            pltpu.VMEM((512, 2 * HALF), F8),
            pltpu.VMEM((UNIT, 3, 2 * HALF, 256), F8),
            pltpu.VMEM((UNIT, 3, 2 * HALF, 256), F8),
            pltpu.VMEM((512, UNIT * 256), BF),
            pltpu.VMEM((512, UNIT * 256), BF),
            pltpu.VMEM((RING, 512, 128), F32),
        ],
        compiler_params=pltpu.CompilerParams(vmem_limit_bytes=40 << 20),
        name="euler_basis",
    )(where, counts, *tables, *queries)


def shift(dz):
    return [(z * RING + y, (z + dz) % RING * RING + y) for z in range(RING) for y in range(RING)]


def trade(sign, pick):
    got = {}
    for k in (2, 1, 3):
        got[k] = lax.ppermute(pick(k), "shk", shift(sign * k))
    return [got[k] for k in (1, 2, 3)]


def spread(current, income):
    nq = current.shape[1]
    rest = jnp.zeros((HALF - DIM - 1, nq), F32)
    one = jnp.ones((1, nq), F32)
    own = jnp.stack([jnp.concatenate([v, one, rest], axis=0) for v in (current, income)])
    return [own] + trade(-1, lambda k: own)


def per_device(savings, wealth, surplus, point_dims, point_levels, point_index, live_count, trans_counts):
    blocks = pack(surplus[0], point_dims, point_levels, point_index, live_count)
    groups = [
        [(2 * x + c) * 16 + z * RING + y for x in range(RING) for y in range(RING)] for c in range(2) for z in range(RING)
    ]
    mine = lax.all_to_all(blocks, ("pts", "shk"), 0, 0, tiled=True, axis_index_groups=groups)
    states = spread(savings[0], wealth[0])
    mine, *states = lax.optimization_barrier((mine, *states))
    tables = (mine, lax.ppermute(mine, "pts", [(i, i ^ 1) for i in range(8)]))
    shock = lax.axis_index("shk")
    where = jnp.stack([shock // RING, shock % RING]).astype(jnp.int32)
    (sums,) = partial_sums(True, where, trans_counts, tables, states)
    parts = [sums] + trade(-1, lambda k: sums)
    queries, current = advance(where, trans_counts, parts, states)
    parts = partial_sums(False, where, trans_counts, tables, queries)
    got = [parts[0]] + trade(1, lambda k: parts[k])
    return finish(where, trans_counts, current, jnp.transpose(wealth, (1, 0, 2)), got)


def solution(mesh):
    return jax.shard_map(
        per_device,
        mesh=mesh,
        in_specs=(
            P("shk", None, "pts"),
            P("shk", None, "pts"),
            P("shk", None, "pts"),
            P("shk", None, "pts"),
            P("shk", None, "pts"),
            P("shk", None, "pts"),
            P("shk", "pts"),
            P(),
        ),
        out_specs=(P("shk", None, "pts"), P("shk", None, "pts")),
        check_vma=False,
    )
```

```python
import functools

import jax
import jax.numpy as jnp
from jax import lax
from jax.experimental import pallas as pl
from jax.experimental.pallas import tpu as pltpu
from jax.sharding import PartitionSpec as P

GAMMA = 2.0
BETA = 0.96
damping = 0.5
DIM = 59
HALF = 64
RING = 4
UNIT = 2
ROWS = 72
WIDTH = 2560
STEP = 0.375 / 32768
BF = jnp.bfloat16
F32 = jnp.float32
F8 = jnp.float8_e4m3fn
SPLIT = 32.0


def pack_kernel(live_ref, surplus_ref, dims_ref, levels_ref, index_ref, o_ref, wide_ref):
    npoints = surplus_ref.shape[1]
    position = lax.broadcasted_iota(jnp.int32, (1, npoints), 1)
    kept = position < live_ref[...]
    wide_ref[0 : 2 * DIM, :] = surplus_ref[...].astype(F32)
    exponent = wide_ref[DIM : 2 * DIM, :] - GAMMA * wide_ref[0:DIM, :]
    steps = jnp.clip(jnp.floor(exponent * (1.0 / STEP) + 0.5), -32767.0, 32767.0)
    wide_ref[0:DIM, :] = steps
    row = lax.broadcasted_iota(jnp.int32, (16, npoints), 0) + (ROWS - 16)
    tail = jnp.where(row < DIM, wide_ref[ROWS - 16 : ROWS, :], 0.0)
    for k in range(3):
        level = levels_ref[k]
        refined = level > 0
        scale = jnp.where(refined, jnp.left_shift(jnp.ones_like(level), level), 0).astype(F32)
        bias = jnp.where(refined, 1 - index_ref[k], 1).astype(F32)
        for place, value in ((DIM + k, dims_ref[k].astype(F32)), (DIM + 3 + k, scale), (DIM + 6 + k, bias)):
            tail = jnp.where(row == place, value, tail)
    wide_ref[ROWS - 16 : ROWS, :] = jnp.where(row == DIM + 9, live_ref[...].astype(F32), tail)
    block = jnp.where(kept, wide_ref[0:ROWS, :], 0.0).astype(jnp.int32).astype(jnp.int16)
    for g in range(o_ref.shape[0]):
        o_ref[g] = block


def pack(surplus, dims, levels, index, live):
    vm = pl.BlockSpec(memory_space=pltpu.VMEM)
    return pl.pallas_call(
        pack_kernel,
        out_shape=jax.ShapeDtypeStruct((16, ROWS, surplus.shape[1]), jnp.int16),
        in_specs=[vm] * 5,
        out_specs=vm,
        scratch_shapes=[pltpu.VMEM((120, surplus.shape[1]), F32)],
        name="pack_tables",
    )(live, surplus, *(jnp.transpose(v, (1, 0, 2)) for v in (dims, levels, index)))


def advance_kernel(where_ref, counts_ref, p0, p1, p2, p3, s0, s1, s2, s3, q0, q1, q2, q3, cur_ref):
    z, y = where_ref[0], where_ref[1]
    row = lax.broadcasted_iota(jnp.int32, (HALF, 128), 0)
    for j, (state, q) in enumerate(((s0, q0), (s1, q1), (s2, q2), (s3, q3))):
        s = lax.rem(z + j, RING) * RING + y
        rowsum = counts_ref[s, 0]
        for t in range(1, RING * RING):
            rowsum += counts_ref[s, t]
        total = (p0[j] + p2[(j - 2) % RING]) + (p1[(j - 1) % RING] + p3[(j - 3) % RING])
        consumption = (BETA * (total / rowsum.astype(F32))) ** (-1.0 / GAMMA)
        share = 1.0 / (1.0 + jnp.exp(consumption - state[1]))
        new = (1.0 - damping) * state[0] + damping * share
        new = jnp.where(row < DIM, new, jnp.where(row == DIM, 1.0, 0.0))
        q[...] = new.astype(BF)
        if j == 0:
            cur_ref[...] = new


def advance(where, counts, parts, states):
    vm = pl.BlockSpec(memory_space=pltpu.VMEM)
    sm = pl.BlockSpec(memory_space=pltpu.SMEM)
    *queries, current = pl.pallas_call(
        advance_kernel,
        out_shape=[jax.ShapeDtypeStruct((HALF, 128), BF)] * RING + [jax.ShapeDtypeStruct((HALF, 128), F32)],
        in_specs=[sm, sm] + [vm] * (2 * RING),
        out_specs=[vm] * (RING + 1),
        compiler_params=pltpu.CompilerParams(vmem_limit_bytes=4 << 20),
        name="advance",
    )(where, counts, *parts, *states)
    return queries, current


def finish_kernel(where_ref, counts_ref, now_ref, income_ref, g0, g1, g2, g3, cur_ref, con_ref):
    total = ((g0[...] + g1[...]) + (g2[...] + g3[...]))[:DIM]
    s = where_ref[0] * RING + where_ref[1]
    rowsum = counts_ref[s, 0]
    for t in range(1, RING * RING):
        rowsum += counts_ref[s, t]
    expect = total / rowsum.astype(F32)
    consumption = (BETA * expect) ** (-1.0 / GAMMA)
    value = income_ref[:, 0, :] - consumption
    share = 1.0 / (1.0 + jnp.exp(-value))
    con_ref[:, 0, :] = consumption
    cur_ref[:, 0, :] = (1.0 - damping) * now_ref[0:DIM, :] + damping * share


def finish(where, counts, current, income, got):
    vm = pl.BlockSpec(memory_space=pltpu.VMEM)
    sm = pl.BlockSpec(memory_space=pltpu.SMEM)
    flat = jax.ShapeDtypeStruct((DIM, 1, current.shape[1]), F32)
    new, consumption = pl.pallas_call(
        finish_kernel,
        out_shape=[flat, flat],
        in_specs=[sm, sm] + [vm] * 6,
        out_specs=[vm, vm],
        compiler_params=pltpu.CompilerParams(vmem_limit_bytes=4 << 20),
        name="finish",
    )(where, counts, current, income, *got)
    return jnp.transpose(new, (1, 0, 2)), jnp.transpose(consumption, (1, 0, 2))


def compact(tab_a, tab_b, unit_ref, o_ref):
    o_ref[...] = jnp.zeros_like(o_ref)
    blocks = [[(tab_ref, x * RING + t) for x in range(RING) for tab_ref in (tab_a, tab_b)] for t in range(RING)]
    lives = [
        [jnp.max(ref[i, ROWS - 8 : ROWS, 0:128].astype(jnp.int32).astype(F32)[DIM + 17 - ROWS]) for ref, i in row]
        for row in blocks
    ]
    offsets = [jnp.int32(0)] * RING
    for n in range(2 * RING):
        for t in range(RING):
            ref, i = blocks[t][n]
            block = ref[i].astype(jnp.int32).astype(F32)
            wide = jnp.concatenate([block, jnp.zeros((ROWS, 128), F32)], axis=1)
            lanes = pl.ds(pl.multiple_of(offsets[t] // 128 * 128, 128), 384)
            o_ref[t, :, lanes] += pltpu.roll(wide, offsets[t] % 128, 1)
            offsets[t] = offsets[t] + lives[t][n].astype(jnp.int32)
    count = jnp.int32(0)
    for t in range(RING):
        for part in range(RING):
            unit_ref[2 * (count + part)] = jnp.int32(t)
            unit_ref[2 * (count + part) + 1] = jnp.int32(512 * part)
        count = count + (offsets[t] + 511) // 512
    unit_ref[2 * count] = jnp.int32(0)
    unit_ref[2 * count + 1] = jnp.int32(2048)
    return count + count % 2


def kernel(
    first, where_ref, counts_ref, tab_a, tab_b, q0, q1, q2, q3, *refs
):
    outs, (qt_ref, sel_a, sel_b, basis_a, basis_b, acc_ref, unit_ref, tab_ref) = refs[:-8], refs[-8:]
    units = compact(tab_a, tab_b, unit_ref, tab_ref)
    z, y = where_ref[0], where_ref[1]
    for j, q in enumerate((q0, q1, q2, q3)):
        whole = (q[0] if first else q[...]).astype(BF).astype(F32)
        whole = jnp.where(lax.broadcasted_iota(jnp.int32, whole.shape, 0) < DIM, whole * SPLIT, whole)
        high = whole.astype(F8).astype(F32)
        qt_ref[pl.ds(j * 128, 128), :] = jnp.concatenate([high, whole - high], axis=0).T.astype(F8)
    row = lax.broadcasted_iota(jnp.int32, (HALF, 256), 0)

    def block(u, b, rows):
        lanes = pl.ds(pl.multiple_of(unit_ref[2 * u + 1] + b * 256, 128), 256)
        return tab_ref[unit_ref[2 * u], rows, lanes]

    def select(u, sel_ref):
        for b in range(UNIT):
            par = block(jnp.minimum(u, units - 1), b, slice(ROWS - 16, ROWS))
            for k in range(3):
                dim = par[3 + k : 4 + k].astype(jnp.int32)
                scale = par[6 + k : 7 + k] * (1.0 / SPLIT)
                bias = par[9 + k : 10 + k]
                table = jnp.where(row == dim, scale, jnp.where(row == DIM, bias, 0.0)).astype(F8)
                sel_ref[b, k, 0:HALF, :] = table
                sel_ref[b, k, HALF : 2 * HALF, :] = table

    def hats(sel_ref, basis_ref):
        for b in range(UNIT):
            basis = None
            for k in range(3):
                left = jnp.dot(qt_ref[...], sel_ref[b, k], preferred_element_type=F32)
                factor = jnp.minimum(left, 2.0 - left)
                factor = jnp.maximum(factor, 0.0) if k < 2 else factor
                basis = factor if basis is None else basis * factor
            basis_ref[:, pl.ds(b * 256, 256)] = jnp.maximum(basis.astype(BF), BF(0.0))

    def halves(steps):
        high = steps.astype(BF)
        return jnp.concatenate([high, (steps - high.astype(F32)).astype(BF)], axis=0)

    def sums(u, basis_ref):
        weights = jnp.concatenate([halves(block(u, b, slice(0, HALF))) for b in range(UNIT)], axis=1)
        acc_ref[unit_ref[2 * u]] += lax.dot_general(
            basis_ref[...], weights, (((1,), (1,)), ((), ())), preferred_element_type=F32
        )

    acc_ref[...] = jnp.zeros_like(acc_ref)
    select(0, sel_a)
    select(1, sel_b)
    hats(sel_a, basis_a)
    select(2, sel_a)

    @pl.loop(0, units // 2 - 1)
    def _(it):
        u = 2 * it + 1
        hats(sel_b, basis_b)
        sums(u - 1, basis_a)
        select(u + 2, sel_b)
        hats(sel_a, basis_a)
        sums(u, basis_b)
        select(u + 3, sel_a)

    hats(sel_b, basis_b)
    sums(units - 2, basis_a)
    sums(units - 1, basis_b)

    for j in range(RING):
        s = lax.rem(z + j, RING) * RING + y
        total = None
        for t in range(RING):
            value = acc_ref[t, pl.ds(j * 128, 128), :]
            count = counts_ref[s, z * RING + t].astype(F32)
            term = count * jnp.exp(STEP * (value + pltpu.roll(value, HALF, 1)))
            total = term if total is None else total + term
        if first:
            outs[0][j] = total.T[:HALF]
        else:
            outs[j][...] = total.T[:HALF]


def partial_sums(first, where, counts, tables, queries):
    vm = pl.BlockSpec(memory_space=pltpu.VMEM)
    sm = pl.BlockSpec(memory_space=pltpu.SMEM)
    if first:
        shapes = [jax.ShapeDtypeStruct((RING, HALF, 128), F32)]
    else:
        shapes = [jax.ShapeDtypeStruct((HALF, 128), F32)] * RING
    return pl.pallas_call(
        functools.partial(kernel, first),
        out_shape=shapes,
        in_specs=[sm, sm] + [vm] * 6,
        out_specs=[vm] * len(shapes),
        scratch_shapes=[
            pltpu.VMEM((512, 2 * HALF), F8),
            pltpu.VMEM((UNIT, 3, 2 * HALF, 256), F8),
            pltpu.VMEM((UNIT, 3, 2 * HALF, 256), F8),
            pltpu.VMEM((512, UNIT * 256), BF),
            pltpu.VMEM((512, UNIT * 256), BF),
            pltpu.VMEM((RING, 512, 128), F32),
            pltpu.SMEM((40,), jnp.int32),
            pltpu.VMEM((RING, ROWS, WIDTH), F32),
        ],
        compiler_params=pltpu.CompilerParams(vmem_limit_bytes=40 << 20),
        name="euler_basis",
    )(where, counts, *tables, *queries)


def shift(dz):
    return [(z * RING + y, (z + dz) % RING * RING + y) for z in range(RING) for y in range(RING)]


def trade(sign, pick):
    got = {}
    for k in (2, 1, 3):
        got[k] = lax.ppermute(pick(k), "shk", shift(sign * k))
    return [got[k] for k in (1, 2, 3)]


def spread(current, income):
    nq = current.shape[1]
    rest = jnp.zeros((HALF - DIM - 1, nq), F32)
    one = jnp.ones((1, nq), F32)
    own = jnp.stack([jnp.concatenate([v, one, rest], axis=0) for v in (current, income)])
    return [own] + trade(-1, lambda k: own)


def per_device(savings, wealth, surplus, point_dims, point_levels, point_index, live_count, trans_counts):
    blocks = pack(surplus[0], point_dims, point_levels, point_index, live_count)
    groups = [
        [(2 * x + c) * 16 + z * RING + y for x in range(RING) for y in range(RING)] for c in range(2) for z in range(RING)
    ]
    mine = lax.all_to_all(blocks, ("pts", "shk"), 0, 0, tiled=True, axis_index_groups=groups)
    states = spread(savings[0], wealth[0])
    mine, *states = lax.optimization_barrier((mine, *states))
    tables = (mine, lax.ppermute(mine, "pts", [(i, i ^ 1) for i in range(8)]))
    shock = lax.axis_index("shk")
    where = jnp.stack([shock // RING, shock % RING]).astype(jnp.int32)
    (sums,) = partial_sums(True, where, trans_counts, tables, states)
    parts = [sums] + trade(-1, lambda k: sums)
    queries, current = advance(where, trans_counts, parts, states)
    parts = partial_sums(False, where, trans_counts, tables, queries)
    got = [parts[0]] + trade(1, lambda k: parts[k])
    return finish(where, trans_counts, current, jnp.transpose(wealth, (1, 0, 2)), got)


def solution(mesh):
    return jax.shard_map(
        per_device,
        mesh=mesh,
        in_specs=(
            P("shk", None, "pts"),
            P("shk", None, "pts"),
            P("shk", None, "pts"),
            P("shk", None, "pts"),
            P("shk", None, "pts"),
            P("shk", None, "pts"),
            P("shk", "pts"),
            P(),
        ),
        out_specs=(P("shk", None, "pts"), P("shk", None, "pts")),
        check_vma=False,
    )
```

```python
import functools

import jax
import jax.numpy as jnp
from jax import lax
from jax.experimental import pallas as pl
from jax.experimental.pallas import tpu as pltpu
from jax.sharding import PartitionSpec as P

GAMMA = 2.0
BETA = 0.96
damping = 0.5
DIM = 59
HALF = 64
RING = 4
UNIT = 2
ROWS = 72
WIDTH = 2560
STEP = 0.375 / 32768
BF = jnp.bfloat16
F32 = jnp.float32
F8 = jnp.float8_e4m3fn
SPLIT = 32.0


def pack_kernel(live_ref, surplus_ref, dims_ref, levels_ref, index_ref, o_ref, wide_ref):
    npoints = surplus_ref.shape[1]
    position = lax.broadcasted_iota(jnp.int32, (1, npoints), 1)
    kept = position < live_ref[...]
    wide_ref[0 : 2 * DIM, :] = surplus_ref[...].astype(F32)
    exponent = wide_ref[DIM : 2 * DIM, :] - GAMMA * wide_ref[0:DIM, :]
    steps = jnp.clip(jnp.floor(exponent * (1.0 / STEP) + 0.5), -32767.0, 32767.0)
    wide_ref[0:DIM, :] = steps
    row = lax.broadcasted_iota(jnp.int32, (16, npoints), 0) + (ROWS - 16)
    tail = jnp.where(row < DIM, wide_ref[ROWS - 16 : ROWS, :], 0.0)
    for k in range(3):
        level = levels_ref[k]
        refined = level > 0
        scale = jnp.where(refined, jnp.left_shift(jnp.ones_like(level), level), 0).astype(F32)
        bias = jnp.where(refined, 1 - index_ref[k], 1).astype(F32)
        for place, value in ((DIM + k, dims_ref[k].astype(F32)), (DIM + 3 + k, scale), (DIM + 6 + k, bias)):
            tail = jnp.where(row == place, value, tail)
    wide_ref[ROWS - 16 : ROWS, :] = jnp.where(row == DIM + 9, live_ref[...].astype(F32), tail)
    block = jnp.where(kept, wide_ref[0:ROWS, :], 0.0).astype(jnp.int32).astype(jnp.int16)
    for g in range(o_ref.shape[0]):
        o_ref[g] = block


def pack(surplus, dims, levels, index, live):
    vm = pl.BlockSpec(memory_space=pltpu.VMEM)
    return pl.pallas_call(
        pack_kernel,
        out_shape=jax.ShapeDtypeStruct((16, ROWS, surplus.shape[1]), jnp.int16),
        in_specs=[vm] * 5,
        out_specs=vm,
        scratch_shapes=[pltpu.VMEM((120, surplus.shape[1]), F32)],
        name="pack_tables",
    )(live, surplus, *(jnp.transpose(v, (1, 0, 2)) for v in (dims, levels, index)))


def advance_kernel(where_ref, counts_ref, p0, p1, p2, p3, s0, s1, s2, s3, q0, q1, q2, q3, cur_ref):
    z, y = where_ref[0], where_ref[1]
    row = lax.broadcasted_iota(jnp.int32, (HALF, 128), 0)
    for j, (state, q) in enumerate(((s0, q0), (s1, q1), (s2, q2), (s3, q3))):
        s = lax.rem(z + j, RING) * RING + y
        rowsum = counts_ref[s, 0]
        for t in range(1, RING * RING):
            rowsum += counts_ref[s, t]
        total = (p0[j] + p2[(j - 2) % RING]) + (p1[(j - 1) % RING] + p3[(j - 3) % RING])
        consumption = (BETA * (total / rowsum.astype(F32))) ** (-1.0 / GAMMA)
        share = 1.0 / (1.0 + jnp.exp(consumption - state[1]))
        new = (1.0 - damping) * state[0] + damping * share
        new = jnp.where(row < DIM, new, jnp.where(row == DIM, 1.0, 0.0))
        q[...] = new.astype(BF)
        if j == 0:
            cur_ref[...] = new


def advance(where, counts, parts, states):
    vm = pl.BlockSpec(memory_space=pltpu.VMEM)
    sm = pl.BlockSpec(memory_space=pltpu.SMEM)
    *queries, current = pl.pallas_call(
        advance_kernel,
        out_shape=[jax.ShapeDtypeStruct((HALF, 128), BF)] * RING + [jax.ShapeDtypeStruct((HALF, 128), F32)],
        in_specs=[sm, sm] + [vm] * (2 * RING),
        out_specs=[vm] * (RING + 1),
        compiler_params=pltpu.CompilerParams(vmem_limit_bytes=4 << 20),
        name="advance",
    )(where, counts, *parts, *states)
    return queries, current


def finish_kernel(where_ref, counts_ref, now_ref, income_ref, g0, g1, g2, g3, cur_ref, con_ref):
    total = ((g0[...] + g1[...]) + (g2[...] + g3[...]))[:DIM]
    s = where_ref[0] * RING + where_ref[1]
    rowsum = counts_ref[s, 0]
    for t in range(1, RING * RING):
        rowsum += counts_ref[s, t]
    expect = total / rowsum.astype(F32)
    consumption = (BETA * expect) ** (-1.0 / GAMMA)
    value = income_ref[:, 0, :] - consumption
    share = 1.0 / (1.0 + jnp.exp(-value))
    con_ref[:, 0, :] = consumption
    cur_ref[:, 0, :] = (1.0 - damping) * now_ref[0:DIM, :] + damping * share


def finish(where, counts, current, income, got):
    vm = pl.BlockSpec(memory_space=pltpu.VMEM)
    sm = pl.BlockSpec(memory_space=pltpu.SMEM)
    flat = jax.ShapeDtypeStruct((DIM, 1, current.shape[1]), F32)
    new, consumption = pl.pallas_call(
        finish_kernel,
        out_shape=[flat, flat],
        in_specs=[sm, sm] + [vm] * 6,
        out_specs=[vm, vm],
        compiler_params=pltpu.CompilerParams(vmem_limit_bytes=4 << 20),
        name="finish",
    )(where, counts, current, income, *got)
    return jnp.transpose(new, (1, 0, 2)), jnp.transpose(consumption, (1, 0, 2))


def compact(tab_a, tab_b, unit_ref, o_ref):
    o_ref[...] = jnp.zeros_like(o_ref)
    blocks = [[(tab_ref, x * RING + t) for x in range(RING) for tab_ref in (tab_a, tab_b)] for t in range(RING)]
    lives = [
        [jnp.max(ref[i, ROWS - 8 : ROWS, 0:128].astype(jnp.int32).astype(F32)[DIM + 17 - ROWS]) for ref, i in row]
        for row in blocks
    ]
    offsets = [jnp.int32(0)] * RING
    for n in range(2 * RING):
        for t in range(RING):
            ref, i = blocks[t][n]
            block = ref[i].astype(jnp.int32).astype(F32)
            wide = jnp.concatenate([block, jnp.zeros((ROWS, 128), F32)], axis=1)
            lanes = pl.ds(pl.multiple_of(offsets[t] // 128 * 128, 128), 384)
            o_ref[t, :, lanes] += pltpu.roll(wide, offsets[t] % 128, 1)
            offsets[t] = offsets[t] + lives[t][n].astype(jnp.int32)
    count = jnp.int32(0)
    for t in range(RING):
        for part in range(RING):
            unit_ref[2 * (count + part)] = jnp.int32(t)
            unit_ref[2 * (count + part) + 1] = jnp.int32(512 * part)
        count = count + (offsets[t] + 511) // 512
    unit_ref[2 * count] = jnp.int32(0)
    unit_ref[2 * count + 1] = jnp.int32(2048)
    unit_ref[39] = count + count % 2


def kernel(
    first, where_ref, counts_ref, one, two, q0, q1, q2, q3, *refs
):
    if first:
        outs, unit_ref, tab_ref = refs[:1], refs[1], refs[2]
        compact(one, two, unit_ref, tab_ref)
    else:
        outs, unit_ref, tab_ref = refs[:4], one, two
    qt_ref, sel_a, sel_b, basis_a, basis_b, acc_ref = refs[-6:]
    units = unit_ref[39]
    z, y = where_ref[0], where_ref[1]
    for j, q in enumerate((q0, q1, q2, q3)):
        whole = (q[0] if first else q[...]).astype(BF).astype(F32)
        whole = jnp.where(lax.broadcasted_iota(jnp.int32, whole.shape, 0) < DIM, whole * SPLIT, whole)
        high = whole.astype(F8).astype(F32)
        qt_ref[pl.ds(j * 128, 128), :] = jnp.concatenate([high, whole - high], axis=0).T.astype(F8)
    row = lax.broadcasted_iota(jnp.int32, (HALF, 256), 0)

    def block(u, b, rows):
        lanes = pl.ds(pl.multiple_of(unit_ref[2 * u + 1] + b * 256, 128), 256)
        return tab_ref[unit_ref[2 * u], rows, lanes]

    def select(u, sel_ref):
        for b in range(UNIT):
            par = block(jnp.minimum(u, units - 1), b, slice(ROWS - 16, ROWS))
            for k in range(3):
                dim = par[3 + k : 4 + k].astype(jnp.int32)
                scale = par[6 + k : 7 + k] * (1.0 / SPLIT)
                bias = par[9 + k : 10 + k]
                table = jnp.where(row == dim, scale, jnp.where(row == DIM, bias, 0.0)).astype(F8)
                sel_ref[b, k, 0:HALF, :] = table
                sel_ref[b, k, HALF : 2 * HALF, :] = table

    def hats(sel_ref, basis_ref):
        for b in range(UNIT):
            basis = None
            for k in range(3):
                left = jnp.dot(qt_ref[...], sel_ref[b, k], preferred_element_type=F32)
                factor = jnp.minimum(left, 2.0 - left)
                factor = jnp.maximum(factor, 0.0) if k < 2 else factor
                basis = factor if basis is None else basis * factor
            basis_ref[:, pl.ds(b * 256, 256)] = jnp.maximum(basis.astype(BF), BF(0.0))

    def halves(steps):
        high = steps.astype(BF)
        return jnp.concatenate([high, (steps - high.astype(F32)).astype(BF)], axis=0)

    def sums(u, basis_ref):
        weights = jnp.concatenate([halves(block(u, b, slice(0, HALF))) for b in range(UNIT)], axis=1)
        acc_ref[unit_ref[2 * u]] += lax.dot_general(
            basis_ref[...], weights, (((1,), (1,)), ((), ())), preferred_element_type=F32
        )

    acc_ref[...] = jnp.zeros_like(acc_ref)
    select(0, sel_a)
    select(1, sel_b)
    hats(sel_a, basis_a)
    select(2, sel_a)

    @pl.loop(0, units // 2 - 1)
    def _(it):
        u = 2 * it + 1
        hats(sel_b, basis_b)
        sums(u - 1, basis_a)
        select(u + 2, sel_b)
        hats(sel_a, basis_a)
        sums(u, basis_b)
        select(u + 3, sel_a)

    hats(sel_b, basis_b)
    sums(units - 2, basis_a)
    sums(units - 1, basis_b)

    for j in range(RING):
        s = lax.rem(z + j, RING) * RING + y
        total = None
        for t in range(RING):
            value = acc_ref[t, pl.ds(j * 128, 128), :]
            count = counts_ref[s, z * RING + t].astype(F32)
            term = count * jnp.exp(STEP * (value + pltpu.roll(value, HALF, 1)))
            total = term if total is None else total + term
        if first:
            outs[0][j] = total.T[:HALF]
        else:
            outs[j][...] = total.T[:HALF]


def partial_sums(first, where, counts, tables, queries):
    vm = pl.BlockSpec(memory_space=pltpu.VMEM)
    sm = pl.BlockSpec(memory_space=pltpu.SMEM)
    if first:
        shapes = [
            jax.ShapeDtypeStruct((RING, HALF, 128), F32),
            jax.ShapeDtypeStruct((40,), jnp.int32),
            jax.ShapeDtypeStruct((RING, ROWS, WIDTH), F32),
        ]
        places = [vm, sm, vm]
    else:
        shapes = [jax.ShapeDtypeStruct((HALF, 128), F32)] * RING
        places = [vm] * RING
    return pl.pallas_call(
        functools.partial(kernel, first),
        out_shape=shapes,
        in_specs=[sm, sm, vm if first else sm] + [vm] * 5,
        out_specs=places,
        scratch_shapes=[
            pltpu.VMEM((512, 2 * HALF), F8),
            pltpu.VMEM((UNIT, 3, 2 * HALF, 256), F8),
            pltpu.VMEM((UNIT, 3, 2 * HALF, 256), F8),
            pltpu.VMEM((512, UNIT * 256), BF),
            pltpu.VMEM((512, UNIT * 256), BF),
            pltpu.VMEM((RING, 512, 128), F32),
        ],
        compiler_params=pltpu.CompilerParams(vmem_limit_bytes=40 << 20),
        name="euler_basis",
    )(where, counts, *tables, *queries)


def shift(dz):
    return [(z * RING + y, (z + dz) % RING * RING + y) for z in range(RING) for y in range(RING)]


def trade(sign, pick):
    got = {}
    for k in (2, 1, 3):
        got[k] = lax.ppermute(pick(k), "shk", shift(sign * k))
    return [got[k] for k in (1, 2, 3)]


def spread(current, income):
    nq = current.shape[1]
    rest = jnp.zeros((HALF - DIM - 1, nq), F32)
    one = jnp.ones((1, nq), F32)
    own = jnp.stack([jnp.concatenate([v, one, rest], axis=0) for v in (current, income)])
    return [own] + trade(-1, lambda k: own)


def per_device(savings, wealth, surplus, point_dims, point_levels, point_index, live_count, trans_counts):
    blocks = pack(surplus[0], point_dims, point_levels, point_index, live_count)
    groups = [
        [(2 * x + c) * 16 + z * RING + y for x in range(RING) for y in range(RING)] for c in range(2) for z in range(RING)
    ]
    mine = lax.all_to_all(blocks, ("pts", "shk"), 0, 0, tiled=True, axis_index_groups=groups)
    states = spread(savings[0], wealth[0])
    mine, *states = lax.optimization_barrier((mine, *states))
    tables = (mine, lax.ppermute(mine, "pts", [(i, i ^ 1) for i in range(8)]))
    shock = lax.axis_index("shk")
    where = jnp.stack([shock // RING, shock % RING]).astype(jnp.int32)
    sums, *tables = partial_sums(True, where, trans_counts, tables, states)
    parts = [sums] + trade(-1, lambda k: sums)
    queries, current = advance(where, trans_counts, parts, states)
    parts = partial_sums(False, where, trans_counts, tables, queries)
    got = [parts[0]] + trade(1, lambda k: parts[k])
    return finish(where, trans_counts, current, jnp.transpose(wealth, (1, 0, 2)), got)


def solution(mesh):
    return jax.shard_map(
        per_device,
        mesh=mesh,
        in_specs=(
            P("shk", None, "pts"),
            P("shk", None, "pts"),
            P("shk", None, "pts"),
            P("shk", None, "pts"),
            P("shk", None, "pts"),
            P("shk", None, "pts"),
            P("shk", "pts"),
            P(),
        ),
        out_specs=(P("shk", None, "pts"), P("shk", None, "pts")),
        check_vma=False,
    )
```

```python
import functools

import jax
import jax.numpy as jnp
from jax import lax
from jax.experimental import pallas as pl
from jax.experimental.pallas import tpu as pltpu
from jax.sharding import PartitionSpec as P

GAMMA = 2.0
BETA = 0.96
damping = 0.5
DIM = 59
HALF = 64
RING = 4
UNIT = 2
ROWS = 72
WIDTH = 2560
STEP = 0.375 / 32768
BF = jnp.bfloat16
F32 = jnp.float32
F8 = jnp.float8_e4m3fn
SPLIT = 32.0


def pack_kernel(live_ref, surplus_ref, dims_ref, levels_ref, index_ref, o_ref, wide_ref):
    npoints = surplus_ref.shape[1]
    position = lax.broadcasted_iota(jnp.int32, (1, npoints), 1)
    kept = position < live_ref[...]
    wide_ref[0 : 2 * DIM, :] = surplus_ref[...].astype(F32)
    exponent = wide_ref[DIM : 2 * DIM, :] - GAMMA * wide_ref[0:DIM, :]
    steps = jnp.clip(jnp.floor(exponent * (1.0 / STEP) + 0.5), -32767.0, 32767.0)
    wide_ref[0:DIM, :] = steps
    row = lax.broadcasted_iota(jnp.int32, (16, npoints), 0) + (ROWS - 16)
    tail = jnp.where(row < DIM, wide_ref[ROWS - 16 : ROWS, :], 0.0)
    for k in range(3):
        level = levels_ref[k]
        refined = level > 0
        scale = jnp.where(refined, jnp.left_shift(jnp.ones_like(level), level), 0).astype(F32)
        bias = jnp.where(refined, 1 - index_ref[k], 1).astype(F32)
        for place, value in ((DIM + k, dims_ref[k].astype(F32)), (DIM + 3 + k, scale), (DIM + 6 + k, bias)):
            tail = jnp.where(row == place, value, tail)
    wide_ref[ROWS - 16 : ROWS, :] = jnp.where(row == DIM + 9, live_ref[...].astype(F32), tail)
    block = jnp.where(kept, wide_ref[0:ROWS, :], 0.0).astype(jnp.int32).astype(jnp.int16)
    for g in range(o_ref.shape[0]):
        o_ref[g] = block


def pack(surplus, dims, levels, index, live):
    vm = pl.BlockSpec(memory_space=pltpu.VMEM)
    return pl.pallas_call(
        pack_kernel,
        out_shape=jax.ShapeDtypeStruct((16, ROWS, surplus.shape[1]), jnp.int16),
        in_specs=[vm] * 5,
        out_specs=vm,
        scratch_shapes=[pltpu.VMEM((120, surplus.shape[1]), F32)],
        name="pack_tables",
    )(live, surplus, *(jnp.transpose(v, (1, 0, 2)) for v in (dims, levels, index)))


def advance_kernel(counts_ref, p0, p1, p2, p3, s0, s1, s2, s3, q0, q1, q2, q3, cur_ref):
    z, y = counts_ref[16, 0], counts_ref[16, 1]
    row = lax.broadcasted_iota(jnp.int32, (HALF, 128), 0)
    for j, (state, q) in enumerate(((s0, q0), (s1, q1), (s2, q2), (s3, q3))):
        s = lax.rem(z + j, RING) * RING + y
        rowsum = counts_ref[s, 0]
        for t in range(1, RING * RING):
            rowsum += counts_ref[s, t]
        total = (p0[j] + p2[(j - 2) % RING]) + (p1[(j - 1) % RING] + p3[(j - 3) % RING])
        consumption = (BETA * (total / rowsum.astype(F32))) ** (-1.0 / GAMMA)
        share = 1.0 / (1.0 + jnp.exp(consumption - state[1]))
        new = (1.0 - damping) * state[0] + damping * share
        new = jnp.where(row < DIM, new, jnp.where(row == DIM, 1.0, 0.0))
        q[...] = new.astype(BF)
        if j == 0:
            cur_ref[...] = new


def advance(counts, parts, states):
    vm = pl.BlockSpec(memory_space=pltpu.VMEM)
    sm = pl.BlockSpec(memory_space=pltpu.SMEM)
    *queries, current = pl.pallas_call(
        advance_kernel,
        out_shape=[jax.ShapeDtypeStruct((HALF, 128), BF)] * RING + [jax.ShapeDtypeStruct((HALF, 128), F32)],
        in_specs=[sm] + [vm] * (2 * RING),
        out_specs=[vm] * (RING + 1),
        compiler_params=pltpu.CompilerParams(vmem_limit_bytes=4 << 20),
        name="advance",
    )(counts, *parts, *states)
    return queries, current


def finish_kernel(counts_ref, now_ref, income_ref, g0, g1, g2, g3, cur_ref, con_ref):
    total = ((g0[...] + g1[...]) + (g2[...] + g3[...]))[:DIM]
    s = counts_ref[16, 0] * RING + counts_ref[16, 1]
    rowsum = counts_ref[s, 0]
    for t in range(1, RING * RING):
        rowsum += counts_ref[s, t]
    expect = total / rowsum.astype(F32)
    consumption = (BETA * expect) ** (-1.0 / GAMMA)
    value = income_ref[:, 0, :] - consumption
    share = 1.0 / (1.0 + jnp.exp(-value))
    con_ref[:, 0, :] = consumption
    cur_ref[:, 0, :] = (1.0 - damping) * now_ref[0:DIM, :] + damping * share


def finish(counts, current, income, got):
    vm = pl.BlockSpec(memory_space=pltpu.VMEM)
    sm = pl.BlockSpec(memory_space=pltpu.SMEM)
    flat = jax.ShapeDtypeStruct((DIM, 1, current.shape[1]), F32)
    new, consumption = pl.pallas_call(
        finish_kernel,
        out_shape=[flat, flat],
        in_specs=[sm] + [vm] * 6,
        out_specs=[vm, vm],
        compiler_params=pltpu.CompilerParams(vmem_limit_bytes=4 << 20),
        name="finish",
    )(counts, current, income, *got)
    return jnp.transpose(new, (1, 0, 2)), jnp.transpose(consumption, (1, 0, 2))


def compact(tab_a, tab_b, unit_ref, o_ref):
    o_ref[...] = jnp.zeros_like(o_ref)
    blocks = [[(tab_ref, x * RING + t) for x in range(RING) for tab_ref in (tab_a, tab_b)] for t in range(RING)]
    lives = [
        [jnp.max(ref[i, ROWS - 8 : ROWS, 0:128].astype(jnp.int32).astype(F32)[DIM + 17 - ROWS]) for ref, i in row]
        for row in blocks
    ]
    offsets = [jnp.int32(0)] * RING
    for n in range(2 * RING):
        for t in range(RING):
            ref, i = blocks[t][n]
            block = ref[i].astype(jnp.int32).astype(F32)
            wide = jnp.concatenate([block, jnp.zeros((ROWS, 128), F32)], axis=1)
            lanes = pl.ds(pl.multiple_of(offsets[t] // 128 * 128, 128), 384)
            o_ref[t, :, lanes] += pltpu.roll(wide, offsets[t] % 128, 1)
            offsets[t] = offsets[t] + lives[t][n].astype(jnp.int32)
    count = jnp.int32(0)
    for t in range(RING):
        for part in range(RING):
            unit_ref[2 * (count + part)] = jnp.int32(t)
            unit_ref[2 * (count + part) + 1] = jnp.int32(512 * part)
        count = count + (offsets[t] + 511) // 512
    unit_ref[2 * count] = jnp.int32(0)
    unit_ref[2 * count + 1] = jnp.int32(2048)
    unit_ref[39] = count + count % 2


def kernel(
    first, counts_ref, one, two, q0, q1, q2, q3, *refs
):
    if first:
        outs, unit_ref, tab_ref = refs[:1], refs[1], refs[2]
        compact(one, two, unit_ref, tab_ref)
    else:
        outs, unit_ref, tab_ref = refs[:4], one, two
    qt_ref, sel_a, sel_b, basis_a, basis_b, acc_ref = refs[-6:]
    units = unit_ref[39]
    z, y = counts_ref[16, 0], counts_ref[16, 1]
    for j, q in enumerate((q0, q1, q2, q3)):
        whole = (q[0] if first else q[...]).astype(BF).astype(F32)
        whole = jnp.where(lax.broadcasted_iota(jnp.int32, whole.shape, 0) < DIM, whole * SPLIT, whole)
        high = whole.astype(F8).astype(F32)
        qt_ref[pl.ds(j * 128, 128), :] = jnp.concatenate([high, whole - high], axis=0).T.astype(F8)
    row = lax.broadcasted_iota(jnp.int32, (HALF, 256), 0)

    def block(u, b, rows):
        lanes = pl.ds(pl.multiple_of(unit_ref[2 * u + 1] + b * 256, 128), 256)
        return tab_ref[unit_ref[2 * u], rows, lanes]

    def select(u, sel_ref):
        for b in range(UNIT):
            par = block(jnp.minimum(u, units - 1), b, slice(ROWS - 16, ROWS))
            for k in range(3):
                dim = par[3 + k : 4 + k].astype(jnp.int32)
                scale = par[6 + k : 7 + k] * (1.0 / SPLIT)
                bias = par[9 + k : 10 + k]
                table = jnp.where(row == dim, scale, jnp.where(row == DIM, bias, 0.0)).astype(F8)
                sel_ref[b, k, 0:HALF, :] = table
                sel_ref[b, k, HALF : 2 * HALF, :] = table

    def hats(sel_ref, basis_ref):
        for b in range(UNIT):
            basis = None
            for k in range(3):
                left = jnp.dot(qt_ref[...], sel_ref[b, k], preferred_element_type=F32)
                factor = jnp.minimum(left, 2.0 - left)
                factor = jnp.maximum(factor, 0.0) if k < 2 else factor
                basis = factor if basis is None else basis * factor
            basis_ref[:, pl.ds(b * 256, 256)] = jnp.maximum(basis.astype(BF), BF(0.0))

    def halves(steps):
        high = steps.astype(BF)
        return jnp.concatenate([high, (steps - high.astype(F32)).astype(BF)], axis=0)

    def sums(u, basis_ref):
        weights = jnp.concatenate([halves(block(u, b, slice(0, HALF))) for b in range(UNIT)], axis=1)
        acc_ref[unit_ref[2 * u]] += lax.dot_general(
            basis_ref[...], weights, (((1,), (1,)), ((), ())), preferred_element_type=F32
        )

    acc_ref[...] = jnp.zeros_like(acc_ref)
    select(0, sel_a)
    select(1, sel_b)
    hats(sel_a, basis_a)
    select(2, sel_a)

    @pl.loop(0, units // 2 - 1)
    def _(it):
        u = 2 * it + 1
        hats(sel_b, basis_b)
        sums(u - 1, basis_a)
        select(u + 2, sel_b)
        hats(sel_a, basis_a)
        sums(u, basis_b)
        select(u + 3, sel_a)

    hats(sel_b, basis_b)
    sums(units - 2, basis_a)
    sums(units - 1, basis_b)

    for j in range(RING):
        s = lax.rem(z + j, RING) * RING + y
        total = None
        for t in range(RING):
            value = acc_ref[t, pl.ds(j * 128, 128), :]
            count = counts_ref[s, z * RING + t].astype(F32)
            term = count * jnp.exp(STEP * (value + pltpu.roll(value, HALF, 1)))
            total = term if total is None else total + term
        if first:
            outs[0][j] = total.T[:HALF]
        else:
            outs[j][...] = total.T[:HALF]


def partial_sums(first, counts, tables, queries):
    vm = pl.BlockSpec(memory_space=pltpu.VMEM)
    sm = pl.BlockSpec(memory_space=pltpu.SMEM)
    if first:
        shapes = [
            jax.ShapeDtypeStruct((RING, HALF, 128), F32),
            jax.ShapeDtypeStruct((40,), jnp.int32),
            jax.ShapeDtypeStruct((RING, ROWS, WIDTH), F32),
        ]
        places = [vm, sm, vm]
    else:
        shapes = [jax.ShapeDtypeStruct((HALF, 128), F32)] * RING
        places = [vm] * RING
    return pl.pallas_call(
        functools.partial(kernel, first),
        out_shape=shapes,
        in_specs=[sm, vm if first else sm] + [vm] * 5,
        out_specs=places,
        scratch_shapes=[
            pltpu.VMEM((512, 2 * HALF), F8),
            pltpu.VMEM((UNIT, 3, 2 * HALF, 256), F8),
            pltpu.VMEM((UNIT, 3, 2 * HALF, 256), F8),
            pltpu.VMEM((512, UNIT * 256), BF),
            pltpu.VMEM((512, UNIT * 256), BF),
            pltpu.VMEM((RING, 512, 128), F32),
        ],
        compiler_params=pltpu.CompilerParams(vmem_limit_bytes=40 << 20),
        name="euler_basis",
    )(counts, *tables, *queries)


def shift(dz):
    return [(z * RING + y, (z + dz) % RING * RING + y) for z in range(RING) for y in range(RING)]


def trade(sign, pick):
    got = {}
    for k in (2, 1, 3):
        got[k] = lax.ppermute(pick(k), "shk", shift(sign * k))
    return [got[k] for k in (1, 2, 3)]


def spread(current, income):
    nq = current.shape[1]
    rest = jnp.zeros((HALF - DIM - 1, nq), F32)
    one = jnp.ones((1, nq), F32)
    own = jnp.stack([jnp.concatenate([v, one, rest], axis=0) for v in (current, income)])
    return [own] + trade(-1, lambda k: own)


def per_device(savings, wealth, surplus, point_dims, point_levels, point_index, live_count, trans_counts):
    blocks = pack(surplus[0], point_dims, point_levels, point_index, live_count)
    groups = [
        [(2 * x + c) * 16 + z * RING + y for x in range(RING) for y in range(RING)] for c in range(2) for z in range(RING)
    ]
    mine = lax.all_to_all(blocks, ("pts", "shk"), 0, 0, tiled=True, axis_index_groups=groups)
    states = spread(savings[0], wealth[0])
    shock = lax.axis_index("shk")
    place = jnp.where(jnp.arange(16) == 0, shock // RING, shock % RING).astype(jnp.int32)
    scalars = jnp.concatenate([trans_counts, place[None]], axis=0)
    mine, scalars, *states = lax.optimization_barrier((mine, scalars, *states))
    tables = (mine, lax.ppermute(mine, "pts", [(i, i ^ 1) for i in range(8)]))
    sums, *tables = partial_sums(True, scalars, tables, states)
    parts = [sums] + trade(-1, lambda k: sums)
    queries, current = advance(scalars, parts, states)
    parts = partial_sums(False, scalars, tables, queries)
    got = [parts[0]] + trade(1, lambda k: parts[k])
    return finish(scalars, current, jnp.transpose(wealth, (1, 0, 2)), got)


def solution(mesh):
    return jax.shard_map(
        per_device,
        mesh=mesh,
        in_specs=(
            P("shk", None, "pts"),
            P("shk", None, "pts"),
            P("shk", None, "pts"),
            P("shk", None, "pts"),
            P("shk", None, "pts"),
            P("shk", None, "pts"),
            P("shk", "pts"),
            P(),
        ),
        out_specs=(P("shk", None, "pts"), P("shk", None, "pts")),
        check_vma=False,
    )
```
